32 devices in a mesh: lat: 4 (over x, core), lon: 8 (over z, y).
Axes of the slice: x: 2, y: 2, z: 4, core: 2. Of those that a mesh axis runs over, the one named last changes fastest.
Arguments:
- start_state: float32 [256, 64, 1024], P('lat', None, 'lon'), may hold values from -6 to 6
- coefficients: float32 [5, 64], replicated, may hold values from 0.05 to 0.35
- w_in: bfloat16 [64, 512], replicated, may hold values from -0.75 to 0.75
- w_out: bfloat16 [512, 64], replicated, may hold values from -0.25 to 0.25
- jacobian: float32 [128, 64], replicated, may hold values from -0.75 to 0.75
- sigma: float32 [128], replicated, may hold values from 0.5 to 2
- obs_values: float32 [8192, 128], P(('lat', 'lon')), may hold values from -6 to 6
- owner: int32 [8192, 1], P(('lat', 'lon')), may hold values from 0 to 31; in each aligned block of 256 rows (0 to 255, 256 to 511, ...) at most 16 rows name the same one
- stencil: int32 [8192, 4], P(('lat', 'lon')), may hold values from 0 to 8191
- counts: int32 [8192], P(('lat', 'lon')), may hold values from 1 to 128
Outputs:
- grad_state: float32 [256, 64, 1024], P('lat', None, 'lon')
- departures: float32 [8192, 128], P(('lat', 'lon'))
- grad_w_in: float32 [64, 512], replicated
- grad_w_out: float32 [512, 64], replicated
The draws below stay inside these ranges and needn't reach their ends.
Inputs may be any that keep to these rules, and one draw needn't show every extreme that they name: owner is the tile's index lat * 8 + lon. Among the rows of one device no tile is named by more than 16 rows, a bound that some block reaches. `stencil`: A cell index inside the owning tile is its row times 128 plus its column.
All inputs are finite; a program needn't handle non-finite values.
Results may differ from the reference program's by a relative error of at most 0.0018.
The reference program's roundings to bfloat16 on the way count: a program that leaves them out, or rounds other values in their place, can miss the bound.
Values sent between devices are 32-bit elements; how exact they have to be, the bound alone decides.
A program may use at most 128 MiB of HBM per device.

```python
import math
import jax
import jax.numpy as jnp
import numpy as np
from jax import lax

HID = 512
CH = 128
TLAT = 64
TLON = 128
FEAT = 64
CAP = 16
OBS_DEV = 256
OBS = 8192
NLAT = 256
NLON = 1024
N_LON = 8
DEVICES = 32


def touch_ends(values, rng, smallest, top_value):
    place = [jax.random.randint(jax.random.fold_in(rng, axis), (), 0, length) for axis, length in enumerate(values.shape)]
    main_axis = values.shape.index(max(values.shape))
    next_to = place[:main_axis] + [(place[main_axis] + 1) % values.shape[main_axis]] + place[main_axis + 1:]
    return values.at[tuple(place)].set(smallest).at[tuple(next_to)].set(top_value)


def steps_of(rng, extent, cuts, smallest, top_value):
    def one(dim, blocks):
        draws = jax.random.uniform(jax.random.fold_in(jax.random.fold_in(rng, 6), dim), (blocks,), jnp.float32, smallest / len(cuts), top_value / len(cuts))
        return jnp.repeat(jnp.exp(draws), extent[dim] // blocks).reshape((-1,) + (1,) * (len(extent) - dim - 1))

    loudness = one(*cuts[0])
    for cut in cuts[1:]:
        loudness = loudness * one(*cut)
    return loudness


def deal_out(key, own, number, rows, number_of, top, bound, skew):
    order = jax.random.permutation(key, number_of)
    crowded, common = load_shares(number_of, rows * top, bound, skew, True), load_shares(number_of, rows * top, bound, skew, False)
    places = jnp.arange(number_of)

    def named(tallies, offset_by):
        used = int((tallies > 0).sum())
        fixed = max(1, used // 4)
        moved = fixed + (places - fixed + offset_by * (used - fixed)) % max(1, number_of - fixed)
        return jnp.zeros((number_of,), jnp.int32).at[order[jnp.where(places < fixed, places, moved)]].set(jnp.asarray(tallies, jnp.int32))

    tallies = jnp.where(number % 4 == 0, named(crowded, number // 4), named(common, number - number // 4 - 1))
    mixed = jax.random.permutation(jax.random.fold_in(own, 3), number_of)
    source_of, sink = mixed[0:number_of // 2 * 2:2], mixed[1:number_of // 2 * 2:2]
    margin = jnp.minimum(tallies[source_of] - 1, bound - tallies[sink]) // 2
    margin = jnp.where((source_of == order[0]) | (sink == order[0]) | (tallies[sink] == 0), 0, jnp.maximum(margin, 0))
    moved = jax.random.randint(jax.random.fold_in(own, 4), (number_of // 2,), 0, 1 << 20) % (margin + 1)
    tallies = tallies.at[source_of].add(-moved).at[sink].add(moved)
    labels = jnp.searchsorted(jnp.cumsum(tallies), jnp.arange(rows * top), side="right").astype(jnp.int32)
    grid = labels.reshape(top, rows).T
    grid = grid[jax.random.permutation(jax.random.fold_in(own, 1), rows)]
    offset_by = jax.random.randint(jax.random.fold_in(own, 2), (rows, 1), 0, top)
    return jnp.take_along_axis(grid, (jnp.arange(top)[None, :] + offset_by) % top, axis=1)


def load_shares(count, total, reach, slope, full):
    weights = [(1 << 20) // math.isqrt(standing ** slope) + 1 for standing in range(1, count + 1)]
    largest = reach if full else min(reach, max(-(-total // count), total * weights[0] // sum(weights)))
    least = 1 if total - largest >= count - 1 else 0
    holding, spare = [largest] + [least] * (count - 1), total - largest - least * (count - 1)
    while spare > 0:
        candidates = [i for i in range(1, count) if holding[i] < largest] or [i for i in range(1, count) if holding[i] < reach]
        pool, budget = sum([weights[i] for i in candidates]), spare
        for i in candidates:
            addition = min(reach - holding[i], max(1, budget * weights[i] // pool), spare)
            holding[i] = holding[i] + addition
            spare = spare - addition
    return np.array(holding)


def noise(stream_key, dims, deviation, most, shards=(), kind=jnp.bfloat16):
    gain = steps_of(stream_key, dims, shards, -0.22, 0.18) if shards else 1.0
    entries = jax.random.normal(stream_key, dims, jnp.float32) * deviation * gain
    return jnp.minimum(jnp.maximum(entries, -most), most).astype(kind)


def setup_inputs(seed: int = 0) -> dict:
    arg_keys = jax.random.split(jax.random.key(seed), 11)
    start_state = noise(arg_keys[0], (NLAT, FEAT, NLON), 1.0, 6.0, ((0, 4), (2, 8)), jnp.float32)
    coefficients = jnp.clip(jax.random.uniform(arg_keys[1], (5, FEAT), jnp.float32, 0.05, 0.35), 0.05, 0.35)
    w_in = noise(arg_keys[2], (FEAT, HID), FEAT ** -0.5, 0.75)
    w_out = noise(arg_keys[3], (HID, FEAT), HID ** -0.5, 0.25)
    jacobian = noise(arg_keys[4], (CH, FEAT), FEAT ** -0.5, 0.75, (), jnp.float32)
    sigma = jnp.clip(jnp.exp(jax.random.uniform(arg_keys[5], (CH,), jnp.float32, math.log(0.5), math.log(2.0))), 0.5, 2.0)
    obs_values = noise(arg_keys[6], (OBS, CH), 1.0, 6.0, ((0, 32),), jnp.float32)
    owner_keys = jax.random.split(jax.random.fold_in(arg_keys[7], 1), OBS // OBS_DEV)
    owner_turns = jax.random.permutation(jax.random.fold_in(arg_keys[7], 3), OBS // OBS_DEV)
    owner = jax.vmap(lambda own, number: deal_out(jax.random.fold_in(arg_keys[7], 2), own, number, OBS_DEV, DEVICES, 1, CAP, 2))(owner_keys, owner_turns).reshape((OBS, 1))
    stencil = touch_ends(jax.random.randint(arg_keys[8], (OBS, 4), 0, TLAT * TLON), jax.random.fold_in(arg_keys[8], 1), 0, (TLAT * TLON) - 1).astype(jnp.int32)
    counts = touch_ends(jax.random.randint(arg_keys[9], (OBS,), 1, CH + 1), jax.random.fold_in(arg_keys[9], 1), 1, CH).astype(jnp.int32)
    return {"start_state": start_state, "coefficients": coefficients, "w_in": w_in, "w_out": w_out, "jacobian": jacobian, "sigma": sigma, "obs_values": obs_values, "owner": owner, "stencil": stencil, "counts": counts}


interp_weights = (0.4, 0.3, 0.2, 0.1)

def group_size(nrows, width, target):
    group = max(1, min(nrows, target // width))
    while nrows % group:
        group -= 1
    return group

def stencil_apply(state, coefficients):
    padded = jnp.pad(state, ((1, 1), (0, 0), (0, 0)))
    scaled = coefficients[:, None, :, None]
    west = jnp.roll(state, 1, axis=2)
    east = jnp.roll(state, -1, axis=2)
    return scaled[0] * state + scaled[1] * padded[:-2] + scaled[2] * padded[2:] + scaled[3] * west + scaled[4] * east

def stencil_adjoint(field, coefficients):
    padded = jnp.pad(field, ((1, 1), (0, 0), (0, 0)))
    scaled = coefficients[:, None, :, None]
    ahead = jnp.roll(field, -1, axis=2)
    behind = jnp.roll(field, 1, axis=2)
    return scaled[0] * field + scaled[1] * padded[2:] + scaled[2] * padded[:-2] + scaled[3] * ahead + scaled[4] * behind

def closure_block(block, w_in, w_out):
    inputs = block.astype(jnp.bfloat16).astype(jnp.float32)
    pre = jnp.einsum('fh,gfw->ghw', w_in.astype(jnp.float32), inputs)
    hidden = jnp.tanh(pre).astype(jnp.bfloat16).astype(jnp.float32)
    return jnp.einsum('hf,ghw->gfw', w_out.astype(jnp.float32), hidden)

def closure_forward(state, w_in, w_out):
    nrows, feat, width = state.shape
    group = group_size(nrows, width, 8192)
    blocks = state.reshape(nrows // group, group, feat, width)
    result = lax.map(lambda block: closure_block(block, w_in, w_out), blocks)
    return result.reshape(nrows, feat, width)

def closure_backward(state, cotangent, w_in, w_out):
    nrows, feat, width = state.shape
    group = group_size(nrows, width, 8192)
    blocks = state.reshape(nrows // group, group, feat, width)
    cot_blocks = cotangent.reshape(nrows // group, group, feat, width)
    w_in32 = w_in.astype(jnp.float32)
    w_out32 = w_out.astype(jnp.float32)

    def one_block(carry, pieces):
        block, cot_block = pieces
        inputs = block.astype(jnp.bfloat16).astype(jnp.float32)
        pre = jnp.einsum('fh,gfw->ghw', w_in32, inputs)
        tanh_pre = jnp.tanh(pre)
        hidden = tanh_pre.astype(jnp.bfloat16).astype(jnp.float32)
        cot_low = cot_block.astype(jnp.bfloat16).astype(jnp.float32)
        grad_out = jnp.einsum('ghw,gfw->hf', hidden, cot_low)
        back_hidden = jnp.einsum('hf,gfw->ghw', w_out32, cot_low)
        back_pre = (back_hidden * (1.0 - tanh_pre * tanh_pre)).astype(jnp.bfloat16).astype(jnp.float32)
        grad_in = jnp.einsum('gfw,ghw->fh', inputs, back_pre)
        back_state = jnp.einsum('fh,ghw->gfw', w_in32, back_pre)
        return ((carry[0] + grad_in, carry[1] + grad_out), back_state)
    init = (jnp.zeros((feat, w_in.shape[1]), jnp.float32), jnp.zeros((w_in.shape[1], feat), jnp.float32))
    totals, back = lax.scan(one_block, init, (blocks, cot_blocks))
    return (back.reshape(nrows, feat, width), totals[0], totals[1])

def reference(start_state, coefficients, w_in, w_out, jacobian, sigma, obs_values, owner, stencil, counts):
    state_one = stencil_apply(start_state, coefficients) + closure_forward(start_state, w_in, w_out)
    state_two = stencil_apply(state_one, coefficients) + closure_forward(state_one, w_in, w_out)
    tile_owner = owner[:, 0]
    row_base = tile_owner // N_LON * TLAT
    col_base = tile_owner % N_LON * TLON
    row_ids = (row_base[:, None] + stencil // TLON).astype(jnp.int32)
    col_ids = (col_base[:, None] + stencil % TLON).astype(jnp.int32)
    interp = interp_weights[0] * state_two[row_ids[:, 0], :, col_ids[:, 0]]
    for corner in range(1, 4):
        interp = interp + interp_weights[corner] * state_two[row_ids[:, corner], :, col_ids[:, corner]]
    evolved = jnp.dot(interp, jacobian.T, precision=lax.Precision.HIGHEST, preferred_element_type=jnp.float32)
    channel = jnp.arange(CH, dtype=jnp.int32)
    used = channel[None, :] < counts[:, None]
    departures = jnp.where(used, (obs_values - evolved) / sigma[None, :], 0.0)
    pulled = jnp.dot(-departures / sigma[None, :], jacobian, precision=lax.Precision.HIGHEST, preferred_element_type=jnp.float32)
    adjoint_two = jnp.zeros_like(state_two)
    for corner in range(4):
        adjoint_two = adjoint_two.at[row_ids[:, corner], :, col_ids[:, corner]].add(interp_weights[corner] * pulled)
    back_one, gin_one, gout_one = closure_backward(state_one, adjoint_two, w_in, w_out)
    adjoint_one = stencil_adjoint(adjoint_two, coefficients) + back_one
    back_zero, gin_zero, gout_zero = closure_backward(start_state, adjoint_one, w_in, w_out)
    grad_state = stencil_adjoint(adjoint_one, coefficients) + back_zero
    scale = 1.0 / math.sqrt(NLAT * NLON)
    return (grad_state, departures, (gin_one + gin_zero) * scale, (gout_one + gout_zero) * scale)
```

```python
import math

import jax
import jax.numpy as jnp
from jax import lax
from jax.experimental import pallas as pl
from jax.experimental.pallas import tpu as pltpu
from jax.sharding import PartitionSpec as P

CAP = 16
CLOSURE_ROWS = 16
BACK_ROWS = 8
PICK_ROWS = 4
SLOT_BLOCK = 512
META = 8
VMEM_LIMIT = 60 * 1024 * 1024
PICK_BYTES = 10 * 1024 * 1024
corner_tenths = (4, 3, 2, 1)
TENTH = 0.1
FORWARD, ADJOINT = (0, 1, 2, 3, 4), (0, 2, 1, 4, 3)
bf16, f32 = jnp.bfloat16, jnp.float32


def mm(a, b):
    return jnp.dot(a, b, preferred_element_type=f32)


def mm_nt(a, b, precision=None):
    return lax.dot_general(
        a, b, (((1,), (1,)), ((), ())), precision=precision, preferred_element_type=f32
    )


def two_parts(x):
    high = x.astype(bf16)
    low = (x - high.astype(f32)).astype(bf16)
    return high, low


def three_parts(x):
    high = x.astype(bf16)
    rest = x - high.astype(f32)
    middle = rest.astype(bf16)
    low = (rest - middle.astype(f32)).astype(bf16)
    return high, middle, low


def turn(x):
    return jnp.transpose(x.astype(f32)).astype(x.dtype)


def picks(local, cells):
    slots = local.shape[1]
    low = local.astype(jnp.int16)
    cell = lax.broadcasted_iota(jnp.int16, (cells, slots), 0)
    zero = jnp.zeros((cells, slots), bf16)
    pick = zero
    for k in range(4):
        same = cell == jnp.broadcast_to(low[k : k + 1], (cells, slots))
        pick = pick + jnp.where(same, jnp.full_like(zero, corner_tenths[k]), zero)
    return pick


def gather_rows(ref, base, count):
    return jnp.concatenate([ref[base + g + 1] for g in range(count)], axis=1).astype(bf16)


def keep_edges(edge, row, i):
    feat, width = row.shape
    lane = lax.broadcasted_iota(jnp.int32, (feat, width), 1)
    moved = pltpu.roll(row, 2 * i + 1, axis=1)
    edge[...] = jnp.where((lane >= 2 * i) & (lane <= 2 * i + 1), moved, edge[...])


def merge_edges(from_west, from_east):
    feat, width = from_west.shape
    lane = lax.broadcasted_iota(jnp.int32, (feat, width), 1)
    return jnp.where(
        lane % 2 == 0, pltpu.roll(from_east, width - 1, axis=1), pltpu.roll(from_west, 1, axis=1)
    )


def stencil_row(rows, sides, weights, i):
    feat, width = rows.shape[1:]
    lane = lax.broadcasted_iota(jnp.int32, (feat, width), 1)
    here = rows[i + 1]
    side = pltpu.roll(sides, width - 1 - 2 * i, axis=1)
    west = jnp.where(lane == 0, side, pltpu.roll(here, 1, axis=1))
    east = jnp.where(lane == width - 1, side, pltpu.roll(here, width - 1, axis=1))
    return (
        weights[0] * here
        + weights[1] * rows[i]
        + weights[2] * rows[i + 2]
        + weights[3] * west
        + weights[4] * east
    )


def remote(src, dst, send, recv, to):
    return pltpu.make_async_remote_copy(
        src_ref=src,
        dst_ref=dst,
        send_sem=send,
        recv_sem=recv,
        device_id=to,
        device_id_type=pl.DeviceIdType.MESH,
    )


def window_kernel(
    start_ref,
    coef_ref,
    w_in_ref,
    w_out_t_ref,
    jac_t_ref,
    sigma_ref,
    obs_ref,
    owner_ref,
    stencil_ref,
    counts_ref,
    grad_ref,
    dep_ref,
    gin_out,
    gout_out,
    x0,
    x1,
    a2,
    a1,
    half,
    edges,
    from_west,
    from_east,
    sides,
    w_in_t,
    w_out,
    slot_row,
    obs_send,
    obs_recv,
    cells,
    pick_store,
    acc,
    parts,
    dep_send,
    dep_recv,
    gin,
    gout,
    rs_send,
    rs_recv,
    ag_send,
    ag_recv,
    load_sem,
    store_sem,
    halo_send,
    halo_recv,
    obs_ssem,
    obs_rsem,
    dep_ssem,
    dep_rsem,
    rs_ssem,
    rs_rsem,
    ag_ssem,
    ag_rsem,
):
    tlat, feat, width = start_ref.shape
    hid = w_in_ref.shape[1]
    rows, channels = obs_ref.shape
    slots = cells.shape[1]
    block = min(slots, SLOT_BLOCK)
    lat, lon = lax.axis_index("lat"), lax.axis_index("lon")
    lats, lons = lax.axis_size("lat"), lax.axis_size("lon")
    devices = lats * lons
    me = lat * lons + lon
    south, north = {"lat": lax.rem(lat + 1, lats)}, {"lat": lax.rem(lat + lats - 1, lats)}
    east, west = {"lon": lax.rem(lon + 1, lons)}, {"lon": lax.rem(lon + lons - 1, lons)}

    load = pltpu.make_async_copy(start_ref, x0.at[pl.ds(1, tlat)], load_sem.at[0])
    load.start()

    def place(index):
        return {"lat": index // lons, "lon": lax.rem(index, lons)}

    barrier = pltpu.get_barrier_semaphore()

    def greet(k, carry):
        pl.semaphore_signal(
            barrier,
            inc=1,
            device_id=place(lax.rem(me + k, devices)),
            device_id_type=pl.DeviceIdType.MESH,
        )
        return carry

    lax.fori_loop(1, devices, greet, 0)

    def swap(source, target, send, recv, spread=False):
        def copy_to(k):
            peer = lax.rem(me + k, devices)
            return remote(
                source if spread else source.at[peer],
                target.at[me],
                send.at[k],
                recv.at[k],
                place(peer),
            )

        def start():
            def body(k, carry):
                copy_to(k).start()
                return carry

            lax.fori_loop(1, devices, body, 0)
            target[me] = source[...] if spread else source[me]

        def finish():
            def body(k, carry):
                copy_to(k).wait()
                return carry

            lax.fori_loop(1, devices, body, 0)

        return start, finish

    def halo(number, field):
        sources = (
            (field.at[tlat], field.at[0], south),
            (field.at[1], field.at[tlat + 1], north),
            (edges.at[number], from_west.at[number], east),
            (edges.at[number], from_east.at[number], west),
        )
        copies = [
            remote(src, dst, halo_send.at[number, k], halo_recv.at[number, k], to)
            for k, (src, dst, to) in enumerate(sources)
        ]

        def start():
            for copy in copies:
                copy.start()

        def finish():
            for copy in copies:
                copy.wait()

            @pl.when(lat == 0)
            def _():
                field[0] = jnp.zeros((feat, width), f32)

            @pl.when(lat == lats - 1)
            def _():
                field[tlat + 1] = jnp.zeros((feat, width), f32)

            sides[...] = merge_edges(from_west[number], from_east[number])

        return start, finish

    owner = owner_ref[...]
    tile = lax.broadcasted_iota(jnp.int32, (devices, rows), 0)
    named = (tile == jnp.broadcast_to(owner, (devices, rows))).astype(f32)
    earlier = (
        lax.broadcasted_iota(jnp.int32, (rows, rows), 0)
        < lax.broadcasted_iota(jnp.int32, (rows, rows), 1)
    ).astype(f32)
    before = mm(named.astype(bf16), earlier.astype(bf16))
    rank = jnp.sum(named * before, axis=0, keepdims=True)
    slot = owner * CAP + rank.astype(jnp.int32)
    slot_row[...] = jnp.broadcast_to(slot, slot_row.shape)
    w_in_t[...] = turn(w_in_ref[...])
    w_out[...] = turn(w_out_t_ref[...])

    obs_parts = jnp.concatenate(three_parts(obs_ref[...]), axis=1)
    stencil = stencil_ref[...]
    filler = jnp.zeros((META - 5, rows), f32)
    meta = jnp.concatenate(
        [
            (stencil // width).astype(f32),
            counts_ref[...].astype(f32),
            filler,
            (stencil % width).astype(f32),
            jnp.zeros((META - 4, rows), f32),
        ],
        axis=0,
    ).astype(bf16)
    per_group = width // CAP
    for s in range(0, slots, block):
        here = jnp.broadcast_to(slot, (block, rows)) - s
        pick = (lax.broadcasted_iota(jnp.int32, (block, rows), 0) == here).astype(f32).astype(bf16)
        wide = mm(pick, obs_parts)
        values = wide[:, :channels] + wide[:, channels : 2 * channels] + wide[:, 2 * channels :]
        for t in range(block // CAP):
            obs_send[s // CAP + t, :CAP] = values[t * CAP : (t + 1) * CAP]
        both = mm_nt(meta, pick)
        scale = jnp.where(
            lax.broadcasted_iota(jnp.int32, (META, block), 0) < 4, float(width), 1.0
        )
        lines = both[:META] * scale + both[META:]
        for t in range(block // CAP):
            g = t // per_group
            line = lines[:, g * width : (g + 1) * width]
            shift = (width - (t % per_group) * CAP) % width
            obs_send[s // CAP + t, CAP:] = pltpu.roll(line, shift, axis=1) if shift else line

    load.wait()
    edges[...] = jnp.zeros_like(edges)

    def first_edges(i, carry):
        keep_edges(edges.at[0], x0[i + 1], i)
        return carry

    lax.fori_loop(0, tlat, first_edges, 0, unroll=4)

    pl.semaphore_wait(barrier, devices - 1)
    halo_0, halo_1 = halo(0, x0), halo(1, x1)
    halo_2, halo_3 = halo(2, a2), halo(3, a1)
    halo_0[0]()
    obs_start, obs_finish = swap(obs_send, obs_recv, obs_ssem, obs_rsem)
    obs_start()

    def weights_of(order):
        turned = jnp.transpose(coef_ref[...])
        return [jnp.broadcast_to(turned[:, k : k + 1], (feat, width)) for k in order]

    def closure(field, out, shift):
        def step(b, carry):
            base = b * CLOSURE_ROWS
            inputs = gather_rows(field, base, CLOSURE_ROWS)
            hidden = jnp.tanh(mm(w_in_t[...], inputs)).astype(bf16)
            result = mm(w_out_t_ref[...], hidden)
            for g in range(CLOSURE_ROWS):
                out[base + g + shift] = result[:, g * width : (g + 1) * width]
            return carry

        lax.fori_loop(0, tlat // CLOSURE_ROWS, step, 0)

    closure(x0, x1, 1)
    halo_0[1]()
    weights = weights_of(FORWARD)

    def finish_one(i, carry):
        row = x1[i + 1] + stencil_row(x0, sides[...], weights, i)
        x1[i + 1] = row
        keep_edges(edges.at[1], row, i)
        return carry

    lax.fori_loop(0, tlat, finish_one, 0, unroll=4)
    halo_1[0]()

    closure(x1, half, 0)
    obs_finish()
    lane = lax.broadcasted_iota(jnp.int32, (META, width), 1)
    for g in range(devices // per_group):
        line = obs_recv[g * per_group, CAP:]
        for t in range(1, per_group):
            moved = pltpu.roll(obs_recv[g * per_group + t, CAP:], t * CAP, axis=1)
            line = jnp.where(lane >= t * CAP, moved, line)
        cells[:, g * width : (g + 1) * width] = line.astype(jnp.int32)
    halo_1[1]()
    acc[...] = jnp.zeros_like(acc)
    keep = pick_store.shape[0] > PICK_ROWS * width

    def finish_two(b, carry):
        base = b * PICK_ROWS
        start = pl.multiple_of(base * width, PICK_ROWS * width)
        out = [
            half[base + g] + stencil_row(x1, sides[...], weights, base + g)
            for g in range(PICK_ROWS)
        ]
        both = jnp.concatenate(two_parts(jnp.concatenate(out, axis=1)), axis=0)
        for s in range(0, slots, block):
            pick = picks(cells[:, s : s + block] - base * width, PICK_ROWS * width)
            if keep:
                pick_store[pl.ds(start, PICK_ROWS * width), s : s + block] = pick
            acc[:, s : s + block] += mm(both, pick)
        return carry

    lax.fori_loop(0, tlat // PICK_ROWS, finish_two, 0)

    jac_t = jac_t_ref[...]
    sigma = sigma_ref[...]
    for s in range(0, slots, block):
        interp = jnp.transpose((acc[:feat, s : s + block] + acc[feat:, s : s + block]) * TENTH)
        evolved = jnp.dot(
            interp, jac_t, precision=lax.Precision.HIGHEST, preferred_element_type=f32
        )
        counts = jnp.transpose(cells[:, s : s + block].astype(f32))[:, 4:5]
        channel = lax.broadcasted_iota(jnp.int32, (block, channels), 1).astype(f32)
        used = channel < jnp.broadcast_to(counts, (block, channels))
        obs = obs_recv[s // CAP : (s + block) // CAP, :CAP].reshape(block, channels)
        departures = jnp.where(used, (obs - evolved) / sigma, 0.0)
        dep_send[s // CAP : (s + block) // CAP] = departures.reshape(block // CAP, CAP, channels)
        pulled = mm_nt(jac_t, -departures / sigma, lax.Precision.HIGHEST)
        parts[:, s : s + block] = jnp.concatenate(two_parts(pulled * TENTH), axis=0)
    dep_start, dep_finish = swap(dep_send, dep_recv, dep_ssem, dep_rsem)
    dep_start()

    def spread(b, carry):
        base = b * PICK_ROWS
        start = pl.multiple_of(base * width, PICK_ROWS * width)
        total = jnp.zeros((2 * feat, PICK_ROWS * width), f32)
        for s in range(0, slots, block):
            if keep:
                pick = pick_store[pl.ds(start, PICK_ROWS * width), s : s + block]
            else:
                pick = picks(cells[:, s : s + block] - base * width, PICK_ROWS * width)
            total = total + mm_nt(parts[:, s : s + block], pick)
        out = total[:feat] + total[feat:]
        for g in range(PICK_ROWS):
            row = out[:, g * width : (g + 1) * width]
            a2[base + g + 1] = row
            keep_edges(edges.at[2], row, base + g)
        return carry

    lax.fori_loop(0, tlat // PICK_ROWS, spread, 0)
    halo_2[0]()

    gin[...] = jnp.zeros_like(gin)
    gout[...] = jnp.zeros_like(gout)

    def closure_back(state, cot_field, out, shift):
        def step(b, carry):
            base = b * BACK_ROWS
            inputs = gather_rows(state, base, BACK_ROWS)
            cot = gather_rows(cot_field, base, BACK_ROWS)
            tanh_pre = jnp.tanh(mm(w_in_t[...], inputs))
            gout[...] += mm_nt(cot, tanh_pre.astype(bf16))
            back_hidden = mm(w_out[...], cot)
            back_pre = (back_hidden * (1.0 - tanh_pre * tanh_pre)).astype(bf16)
            gin[...] += mm_nt(inputs, back_pre)
            back = mm(w_in_ref[...], back_pre)
            for g in range(BACK_ROWS):
                out[base + g + shift] = back[:, g * width : (g + 1) * width]
            return carry

        lax.fori_loop(0, tlat // BACK_ROWS, step, 0)

    closure_back(x1, a2, a1, 1)
    halo_2[1]()
    weights = weights_of(ADJOINT)

    def finish_adjoint(i, carry):
        row = a1[i + 1] + stencil_row(a2, sides[...], weights, i)
        a1[i + 1] = row
        keep_edges(edges.at[3], row, i)
        return carry

    lax.fori_loop(0, tlat, finish_adjoint, 0, unroll=4)
    halo_3[0]()

    dep_finish()
    slot_column = jnp.transpose(slot_row[...].astype(f32))[:, :1].astype(jnp.int32)
    total = jnp.zeros((rows, 3 * channels), f32)
    for s in range(0, slots, block):
        here = jnp.broadcast_to(slot_column, (rows, block)) - s
        pick = (lax.broadcasted_iota(jnp.int32, (rows, block), 1) == here).astype(f32).astype(bf16)
        values = dep_recv[s // CAP : (s + block) // CAP].reshape(block, channels)
        total = total + mm(pick, jnp.concatenate(three_parts(values), axis=1))
    dep_ref[...] = (
        total[:, :channels] + total[:, channels : 2 * channels] + total[:, 2 * channels :]
    )

    closure_back(x0, a1, half, 0)
    grads = jnp.concatenate([gin[...], gout[...]], axis=0)
    stacked = jnp.concatenate(
        [grads[:, c : c + width] for c in range(0, hid, width)], axis=0
    )
    rs_send[...] = stacked.reshape(rs_send.shape)
    rs_start, rs_finish = swap(rs_send, rs_recv, rs_ssem, rs_rsem)
    rs_start()
    halo_3[1]()

    def finish_start(i, carry):
        half[i] = half[i] + stencil_row(a1, sides[...], weights, i)
        return carry

    chunk = tlat // store_sem.shape[0]
    stores = []
    for c in range(store_sem.shape[0]):
        lax.fori_loop(c * chunk, (c + 1) * chunk, finish_start, 0, unroll=4)
        part = pl.ds(c * chunk, chunk)
        stores.append(pltpu.make_async_copy(half.at[part], grad_ref.at[part], store_sem.at[c]))
        stores[-1].start()

    rs_finish()
    scale = 1.0 / math.sqrt(tlat * lats * width * lons)
    ag_send[...] = jnp.sum(rs_recv[...], axis=0) * scale
    ag_start, ag_finish = swap(ag_send, ag_recv, ag_ssem, ag_rsem, spread=True)
    ag_start()
    for store in stores:
        store.wait()
    ag_finish()
    whole = ag_recv[...].reshape(hid // width, 2 * feat, width)
    for c in range(hid // width):
        gin_out[:, c * width : (c + 1) * width] = whole[c, :feat]
        gout_out[:, c * width : (c + 1) * width] = whole[c, feat:]


def on_device(
    start_state, coefficients, w_in, w_out, jacobian, sigma, obs_values, owner, stencil, counts
):
    tlat, feat, width = start_state.shape
    rows, channels = obs_values.shape
    hid = w_in.shape[1]
    devices = lax.axis_size("lat") * lax.axis_size("lon")
    slots = devices * CAP
    cell_count = tlat * width
    assert cell_count <= 1 << 15 and 2 * tlat <= width and max(width, channels) <= 256
    assert (hid * 2 * feat) % (devices * width) == 0 and width % CAP == 0
    assert channels == width and hid % width == 0
    share = hid * 2 * feat // (devices * width)
    keep = cell_count * slots * 2 <= PICK_BYTES
    field = pltpu.VMEM((tlat + 2, feat, width), f32)
    shape = lambda *dims: jax.ShapeDtypeStruct(dims, f32)
    vmem = pl.BlockSpec(memory_space=pltpu.VMEM)
    hbm = pl.BlockSpec(memory_space=pl.ANY)
    dma = pltpu.SemaphoreType.DMA
    args = (
        start_state,
        coefficients,
        w_in,
        w_out.T,
        jacobian.T,
        sigma.reshape(1, channels),
        obs_values,
        owner.T,
        stencil.T,
        counts.reshape(1, rows),
    )
    grad_state, departures, grad_w_in, grad_w_out_t = pl.pallas_call(
        window_kernel,
        out_shape=(
            shape(tlat, feat, width),
            shape(rows, channels),
            shape(feat, hid),
            shape(feat, hid),
        ),
        in_specs=[hbm] + [vmem] * (len(args) - 1),
        out_specs=(hbm, vmem, vmem, vmem),
        scratch_shapes=[field] * 4
        + [
            pltpu.VMEM((tlat, feat, width), f32),
            pltpu.VMEM((4, feat, width), f32),
            pltpu.VMEM((4, feat, width), f32),
            pltpu.VMEM((4, feat, width), f32),
            pltpu.VMEM((feat, width), f32),
            pltpu.VMEM((hid, feat), bf16),
            pltpu.VMEM((hid, feat), bf16),
            pltpu.VMEM((8, rows), jnp.int32),
            pltpu.VMEM((devices, CAP + META, width), f32),
            pltpu.VMEM((devices, CAP + META, width), f32),
            pltpu.VMEM((META, slots), jnp.int32),
            pltpu.VMEM((cell_count, slots) if keep else (PICK_ROWS, slots), bf16),
            pltpu.VMEM((2 * feat, slots), f32),
            pltpu.VMEM((2 * feat, slots), bf16),
            pltpu.VMEM((devices, CAP, channels), f32),
            pltpu.VMEM((devices, CAP, channels), f32),
            pltpu.VMEM((feat, hid), f32),
            pltpu.VMEM((feat, hid), f32),
            pltpu.VMEM((devices, share, width), f32),
            pltpu.VMEM((devices, share, width), f32),
            pltpu.VMEM((share, width), f32),
            pltpu.VMEM((devices, share, width), f32),
            dma((1,)),
            dma((4,)),
            dma((4, 4)),
            dma((4, 4)),
        ]
        + [dma((devices,))] * 8,
        compiler_params=pltpu.CompilerParams(
            collective_id=0, has_side_effects=True, vmem_limit_bytes=VMEM_LIMIT
        ),
    )(*args)
    return grad_state, departures, grad_w_in, grad_w_out_t.T


def solution(mesh):
    return jax.shard_map(
        on_device,
        mesh=mesh,
        in_specs=(
            P("lat", None, "lon"),
            P(),
            P(),
            P(),
            P(),
            P(),
            P(("lat", "lon"), None),
            P(("lat", "lon"), None),
            P(("lat", "lon"), None),
            P(("lat", "lon")),
        ),
        out_specs=(P("lat", None, "lon"), P(("lat", "lon"), None), P(), P()),
        check_vma=False,
    )
```

```python
import math

import jax
import jax.numpy as jnp
from jax import lax
from jax.experimental import pallas as pl
from jax.experimental.pallas import tpu as pltpu
from jax.sharding import PartitionSpec as P

CAP = 16
CLOSURE_ROWS = 16
BACK_ROWS = 8
PICK_ROWS = 4
PASS_ROWS = 16
SLOT_BLOCK = 512
META = 8
VMEM_LIMIT = 60 * 1024 * 1024
PICK_BYTES = 10 * 1024 * 1024
corner_tenths = (4, 3, 2, 1)
TENTH = 0.1
FORWARD, ADJOINT = (0, 1, 2, 3, 4), (0, 2, 1, 4, 3)
bf16, f32 = jnp.bfloat16, jnp.float32


def mm(a, b):
    return jnp.dot(a, b, preferred_element_type=f32)


def mm_nt(a, b, precision=None):
    return lax.dot_general(
        a, b, (((1,), (1,)), ((), ())), precision=precision, preferred_element_type=f32
    )


def two_parts(x):
    high = x.astype(bf16)
    low = (x - high.astype(f32)).astype(bf16)
    return high, low


def three_parts(x):
    high = x.astype(bf16)
    rest = x - high.astype(f32)
    middle = rest.astype(bf16)
    low = (rest - middle.astype(f32)).astype(bf16)
    return high, middle, low


def turn(x):
    return jnp.transpose(x.astype(f32)).astype(x.dtype)


def picks(local, cells):
    slots = local.shape[1]
    low = local.astype(jnp.int16)
    cell = lax.broadcasted_iota(jnp.int16, (cells, slots), 0)
    zero = jnp.zeros((cells, slots), bf16)
    pick = zero
    for k in range(4):
        same = cell == jnp.broadcast_to(low[k : k + 1], (cells, slots))
        pick = pick + jnp.where(same, jnp.full_like(zero, corner_tenths[k]), zero)
    return pick


def gather_rows(ref, base, count):
    return jnp.concatenate([ref[base + g + 1] for g in range(count)], axis=1).astype(bf16)


def merge_edges(from_west, from_east):
    feat, width = from_west.shape
    lane = lax.broadcasted_iota(jnp.int32, (feat, width), 1)
    return jnp.where(
        lane % 2 == 0, pltpu.roll(from_east, width - 1, axis=1), pltpu.roll(from_west, 1, axis=1)
    )


def edge_pass(field, edge):
    rows, feat, width = field.shape
    pair = lax.broadcasted_iota(jnp.int32, (8, width), 1) >> 1

    def step(b, carry):
        part = pl.ds(pl.multiple_of(b * 8, 8), 8)
        kept = []
        for first in range(0, rows - 2, PASS_ROWS):
            total = jnp.zeros((8, width), f32)
            for i in range(first, first + PASS_ROWS):
                moved = pltpu.roll(field[i + 1, part], 2 * i + 1, axis=1)
                total = jnp.where(pair == i, moved, total)
            kept.append(total)
        edge[part] = sum(kept)
        return carry

    lax.fori_loop(0, feat // 8, step, 0)


def shift_matrix(width):
    row = lax.broadcasted_iota(jnp.int32, (2 * width, 2 * width), 0) % width
    column = lax.broadcasted_iota(jnp.int32, (2 * width, 2 * width), 1)
    taken = jnp.where(column < width, column - 1, column - width + 1)
    return (row == taken).astype(f32).astype(bf16)


def stencil_pass(field, sides, weights, shifts, order, base, out, edge=None, shift=0):
    rows, feat, width = field.shape
    lane = lax.broadcasted_iota(jnp.int32, (8, width), 1)
    pair = lane >> 1

    def step(b, carry):
        part = pl.ds(pl.multiple_of(b * 8, 8), 8)
        centre, north, south, west, east = [weights[k, part] for k in order]
        ends = jnp.where(lane == 0, west, jnp.where(lane == width - 1, east, 0.0))
        side = sides[part]
        inner = field[1 : rows - 1, part].reshape((rows - 2) * 8, width)
        beside = mm(jnp.concatenate(two_parts(inner), axis=1), shifts[...])

        def read(start):
            fresh = range(start, min(start + PASS_ROWS, rows - 2))
            return [field[i + 2, part] for i in fresh], [base[i + shift, part] for i in fresh]

        before, here = field[0, part], field[1, part]
        kept = []
        ready = read(0)
        for start in range(0, rows - 2, PASS_ROWS):
            afters, bases = ready
            ready = read(start + PASS_ROWS)
            results = []
            for i, after, total in zip(range(start, start + PASS_ROWS), afters, bases):
                near = beside[i * 8 : (i + 1) * 8]
                results.append(
                    total
                    + centre * here
                    + north * before
                    + south * after
                    + west * near[:, :width]
                    + east * near[:, width:]
                    + ends * pltpu.roll(side, width - 1 - 2 * i, axis=1)
                )
                before, here = here, after
            for g, row in enumerate(results):
                out[start + g + shift, part] = row
            if edge is not None:
                total = jnp.zeros((8, width), f32)
                for g, row in enumerate(results):
                    i = start + g
                    total = jnp.where(pair == i, pltpu.roll(row, 2 * i + 1, axis=1), total)
                kept.append(total)
        if edge is not None:
            edge[part] = sum(kept)
        return carry

    lax.fori_loop(0, feat // 8, step, 0)


def remote(src, dst, send, recv, to):
    return pltpu.make_async_remote_copy(
        src_ref=src,
        dst_ref=dst,
        send_sem=send,
        recv_sem=recv,
        device_id=to,
        device_id_type=pl.DeviceIdType.MESH,
    )


def window_kernel(
    start_ref,
    coef_ref,
    w_in_ref,
    w_out_t_ref,
    jac_t_ref,
    sigma_ref,
    obs_ref,
    owner_ref,
    stencil_ref,
    counts_ref,
    grad_ref,
    dep_ref,
    gin_out,
    gout_out,
    x0,
    x1,
    a2,
    a1,
    half,
    edges,
    from_west,
    from_east,
    sides,
    weights,
    shifts,
    tanh_0,
    tanh_1,
    w_in_t,
    w_out,
    slot_row,
    obs_send,
    obs_recv,
    cells,
    pick_store,
    acc,
    parts,
    dep_send,
    dep_recv,
    gin,
    gout,
    rs_send,
    rs_recv,
    ag_send,
    ag_recv,
    load_sem,
    store_sem,
    halo_send,
    halo_recv,
    obs_ssem,
    obs_rsem,
    dep_ssem,
    dep_rsem,
    rs_ssem,
    rs_rsem,
    ag_ssem,
    ag_rsem,
):
    tlat, feat, width = start_ref.shape
    hid = w_in_ref.shape[1]
    rows, channels = obs_ref.shape
    slots = cells.shape[1]
    block = min(slots, SLOT_BLOCK)
    lat, lon = lax.axis_index("lat"), lax.axis_index("lon")
    lats, lons = lax.axis_size("lat"), lax.axis_size("lon")
    devices = lats * lons
    me = lat * lons + lon
    south, north = {"lat": lax.rem(lat + 1, lats)}, {"lat": lax.rem(lat + lats - 1, lats)}
    east, west = {"lon": lax.rem(lon + 1, lons)}, {"lon": lax.rem(lon + lons - 1, lons)}

    load = pltpu.make_async_copy(start_ref, x0.at[pl.ds(1, tlat)], load_sem.at[0])
    load.start()

    def place(index):
        return {"lat": index // lons, "lon": lax.rem(index, lons)}

    barrier = pltpu.get_barrier_semaphore()

    def greet(k, carry):
        pl.semaphore_signal(
            barrier,
            inc=1,
            device_id=place(lax.rem(me + k, devices)),
            device_id_type=pl.DeviceIdType.MESH,
        )
        return carry

    lax.fori_loop(1, devices, greet, 0)

    def swap(source, target, send, recv, spread=False):
        def copy_to(k):
            peer = lax.rem(me + k, devices)
            return remote(
                source if spread else source.at[peer],
                target.at[me],
                send.at[k],
                recv.at[k],
                place(peer),
            )

        def start():
            def body(k, carry):
                copy_to(k).start()
                return carry

            lax.fori_loop(1, devices, body, 0)
            target[me] = source[...] if spread else source[me]

        def finish():
            def body(k, carry):
                copy_to(k).wait()
                return carry

            lax.fori_loop(1, devices, body, 0)

        return start, finish

    def halo(number, field):
        sources = (
            (field.at[tlat], field.at[0], south),
            (field.at[1], field.at[tlat + 1], north),
            (edges.at[number], from_west.at[number], east),
            (edges.at[number], from_east.at[number], west),
        )
        copies = [
            remote(src, dst, halo_send.at[number, k], halo_recv.at[number, k], to)
            for k, (src, dst, to) in enumerate(sources)
        ]

        def start():
            for copy in copies:
                copy.start()

        def finish():
            for copy in copies:
                copy.wait()

            @pl.when(lat == 0)
            def _():
                field[0] = jnp.zeros((feat, width), f32)

            @pl.when(lat == lats - 1)
            def _():
                field[tlat + 1] = jnp.zeros((feat, width), f32)

            sides[...] = merge_edges(from_west[number], from_east[number])

        return start, finish

    owner = owner_ref[...]
    tile = lax.broadcasted_iota(jnp.int32, (devices, rows), 0)
    named = (tile == jnp.broadcast_to(owner, (devices, rows))).astype(f32)
    earlier = (
        lax.broadcasted_iota(jnp.int32, (rows, rows), 0)
        < lax.broadcasted_iota(jnp.int32, (rows, rows), 1)
    ).astype(f32)
    before = mm(named.astype(bf16), earlier.astype(bf16))
    rank = jnp.sum(named * before, axis=0, keepdims=True)
    slot = owner * CAP + rank.astype(jnp.int32)
    slot_row[...] = jnp.broadcast_to(slot, slot_row.shape)
    w_in_t[...] = turn(w_in_ref[...])
    w_out[...] = turn(w_out_t_ref[...])

    obs_parts = jnp.concatenate(three_parts(obs_ref[...]), axis=1)
    stencil = stencil_ref[...]
    filler = jnp.zeros((META - 5, rows), f32)
    meta = jnp.concatenate(
        [
            (stencil // width).astype(f32),
            counts_ref[...].astype(f32),
            filler,
            (stencil % width).astype(f32),
            jnp.zeros((META - 4, rows), f32),
        ],
        axis=0,
    ).astype(bf16)
    per_group = width // CAP
    for s in range(0, slots, block):
        here = jnp.broadcast_to(slot, (block, rows)) - s
        pick = (lax.broadcasted_iota(jnp.int32, (block, rows), 0) == here).astype(f32).astype(bf16)
        wide = mm(pick, obs_parts)
        values = wide[:, :channels] + wide[:, channels : 2 * channels] + wide[:, 2 * channels :]
        for t in range(block // CAP):
            obs_send[s // CAP + t, :CAP] = values[t * CAP : (t + 1) * CAP]
        both = mm_nt(meta, pick)
        scale = jnp.where(
            lax.broadcasted_iota(jnp.int32, (META, block), 0) < 4, float(width), 1.0
        )
        lines = both[:META] * scale + both[META:]
        for t in range(block // CAP):
            g = t // per_group
            line = lines[:, g * width : (g + 1) * width]
            shift = (width - (t % per_group) * CAP) % width
            obs_send[s // CAP + t, CAP:] = pltpu.roll(line, shift, axis=1) if shift else line

    load.wait()
    edge_pass(x0, edges.at[0])
    shifts[...] = shift_matrix(width)
    turned = jnp.transpose(coef_ref[...])
    for k in range(5):
        weights[k] = jnp.broadcast_to(turned[:, k : k + 1], (feat, width))

    pl.semaphore_wait(barrier, devices - 1)
    halo_0, halo_1 = halo(0, x0), halo(1, x1)
    halo_2, halo_3 = halo(2, a2), halo(3, a1)
    halo_0[0]()
    obs_start, obs_finish = swap(obs_send, obs_recv, obs_ssem, obs_rsem)
    obs_start()

    per_step = CLOSURE_ROWS // BACK_ROWS

    def closure(field, kept, out, shift):
        def step(b, carry):
            base = b * CLOSURE_ROWS
            inputs = gather_rows(field, base, CLOSURE_ROWS)
            tanh_pre = jnp.tanh(mm(w_in_t[...], inputs))
            for g in range(per_step):
                columns = slice(g * BACK_ROWS * width, (g + 1) * BACK_ROWS * width)
                kept[b * per_step + g] = tanh_pre[:, columns]
            result = mm(w_out_t_ref[...], tanh_pre.astype(bf16))
            for g in range(CLOSURE_ROWS):
                out[base + g + shift] = result[:, g * width : (g + 1) * width]
            return carry

        lax.fori_loop(0, tlat // CLOSURE_ROWS, step, 0)

    closure(x0, tanh_0, x1, 1)
    halo_0[1]()
    stencil_pass(x0, sides, weights, shifts, FORWARD, x1, x1, edges.at[1], 1)
    halo_1[0]()

    closure(x1, tanh_1, half, 0)
    obs_finish()
    lane = lax.broadcasted_iota(jnp.int32, (META, width), 1)
    for g in range(devices // per_group):
        line = obs_recv[g * per_group, CAP:]
        for t in range(1, per_group):
            moved = pltpu.roll(obs_recv[g * per_group + t, CAP:], t * CAP, axis=1)
            line = jnp.where(lane >= t * CAP, moved, line)
        cells[:, g * width : (g + 1) * width] = line.astype(jnp.int32)
    halo_1[1]()
    stencil_pass(x1, sides, weights, shifts, FORWARD, half, half)
    acc[...] = jnp.zeros_like(acc)
    keep = pick_store.shape[0] > 1

    def interpolate(b, carry):
        base = b * PICK_ROWS
        state = jnp.concatenate([half[base + g] for g in range(PICK_ROWS)], axis=1)
        both = jnp.concatenate(two_parts(state), axis=0)
        for s in range(0, slots, block):
            pick = picks(cells[:, s : s + block] - base * width, PICK_ROWS * width)
            if keep:
                pick_store[b, :, s : s + block] = pick
            acc[:, s : s + block] += mm(both, pick)
        return carry

    lax.fori_loop(0, tlat // PICK_ROWS, interpolate, 0)

    jac_t = jac_t_ref[...]
    sigma = sigma_ref[...]
    for s in range(0, slots, block):
        interp = jnp.transpose((acc[:feat, s : s + block] + acc[feat:, s : s + block]) * TENTH)
        evolved = jnp.dot(
            interp, jac_t, precision=lax.Precision.HIGHEST, preferred_element_type=f32
        )
        counts = jnp.transpose(cells[:, s : s + block].astype(f32))[:, 4:5]
        channel = lax.broadcasted_iota(jnp.int32, (block, channels), 1).astype(f32)
        used = channel < jnp.broadcast_to(counts, (block, channels))
        obs = obs_recv[s // CAP : (s + block) // CAP, :CAP].reshape(block, channels)
        departures = jnp.where(used, (obs - evolved) / sigma, 0.0)
        dep_send[s // CAP : (s + block) // CAP] = departures.reshape(block // CAP, CAP, channels)
        pulled = mm_nt(jac_t, -departures / sigma, lax.Precision.HIGHEST)
        parts[:, s : s + block] = jnp.concatenate(two_parts(pulled * TENTH), axis=0)
    dep_start, dep_finish = swap(dep_send, dep_recv, dep_ssem, dep_rsem)
    dep_start()

    def spread(b, carry):
        base = b * PICK_ROWS
        total = jnp.zeros((2 * feat, PICK_ROWS * width), f32)
        for s in range(0, slots, block):
            if keep:
                pick = pick_store[b, :, s : s + block]
            else:
                pick = picks(cells[:, s : s + block] - base * width, PICK_ROWS * width)
            total = total + mm_nt(parts[:, s : s + block], pick)
        out = total[:feat] + total[feat:]
        for g in range(PICK_ROWS):
            a2[base + g + 1] = out[:, g * width : (g + 1) * width]
        return carry

    lax.fori_loop(0, tlat // PICK_ROWS, spread, 0)
    edge_pass(a2, edges.at[2])
    halo_2[0]()

    gin[...] = jnp.zeros_like(gin)
    gout[...] = jnp.zeros_like(gout)

    def closure_back(state, kept, cot_field, out, shift):
        def step(b, carry):
            base = b * BACK_ROWS
            inputs = gather_rows(state, base, BACK_ROWS)
            cot = gather_rows(cot_field, base, BACK_ROWS)
            tanh_pre = kept[b]
            gout[...] += mm_nt(cot, tanh_pre.astype(bf16))
            back_hidden = mm(w_out[...], cot)
            back_pre = (back_hidden * (1.0 - tanh_pre * tanh_pre)).astype(bf16)
            gin[...] += mm_nt(inputs, back_pre)
            back = mm(w_in_ref[...], back_pre)
            for g in range(BACK_ROWS):
                out[base + g + shift] = back[:, g * width : (g + 1) * width]
            return carry

        lax.fori_loop(0, tlat // BACK_ROWS, step, 0)

    closure_back(x1, tanh_1, a2, a1, 1)
    halo_2[1]()
    stencil_pass(a2, sides, weights, shifts, ADJOINT, a1, a1, edges.at[3], 1)
    halo_3[0]()

    dep_finish()
    slot_column = jnp.transpose(slot_row[...].astype(f32))[:, :1].astype(jnp.int32)
    total = jnp.zeros((rows, 3 * channels), f32)
    for s in range(0, slots, block):
        here = jnp.broadcast_to(slot_column, (rows, block)) - s
        pick = (lax.broadcasted_iota(jnp.int32, (rows, block), 1) == here).astype(f32).astype(bf16)
        values = dep_recv[s // CAP : (s + block) // CAP].reshape(block, channels)
        total = total + mm(pick, jnp.concatenate(three_parts(values), axis=1))
    dep_ref[...] = (
        total[:, :channels] + total[:, channels : 2 * channels] + total[:, 2 * channels :]
    )

    closure_back(x0, tanh_0, a1, half, 0)
    grads = jnp.concatenate([gin[...], gout[...]], axis=0)
    stacked = jnp.concatenate(
        [grads[:, c : c + width] for c in range(0, hid, width)], axis=0
    )
    rs_send[...] = stacked.reshape(rs_send.shape)
    rs_start, rs_finish = swap(rs_send, rs_recv, rs_ssem, rs_rsem)
    rs_start()
    halo_3[1]()

    stencil_pass(a1, sides, weights, shifts, ADJOINT, half, half)
    store = pltpu.make_async_copy(half, grad_ref, store_sem.at[0])
    store.start()

    rs_finish()
    scale = 1.0 / math.sqrt(tlat * lats * width * lons)
    ag_send[...] = jnp.sum(rs_recv[...], axis=0) * scale
    ag_start, ag_finish = swap(ag_send, ag_recv, ag_ssem, ag_rsem, spread=True)
    ag_start()
    store.wait()
    ag_finish()
    whole = ag_recv[...].reshape(hid // width, 2 * feat, width)
    for c in range(hid // width):
        gin_out[:, c * width : (c + 1) * width] = whole[c, :feat]
        gout_out[:, c * width : (c + 1) * width] = whole[c, feat:]


def on_device(
    start_state, coefficients, w_in, w_out, jacobian, sigma, obs_values, owner, stencil, counts
):
    tlat, feat, width = start_state.shape
    rows, channels = obs_values.shape
    hid = w_in.shape[1]
    devices = lax.axis_size("lat") * lax.axis_size("lon")
    slots = devices * CAP
    cell_count = tlat * width
    assert cell_count <= 1 << 15 and 2 * tlat <= width and max(width, channels) <= 256
    assert (hid * 2 * feat) % (devices * width) == 0 and width % CAP == 0
    assert channels == width and hid % width == 0
    share = hid * 2 * feat // (devices * width)
    keep = cell_count * slots * 2 <= PICK_BYTES
    field = pltpu.VMEM((tlat + 2, feat, width), f32)
    shape = lambda *dims: jax.ShapeDtypeStruct(dims, f32)
    vmem = pl.BlockSpec(memory_space=pltpu.VMEM)
    hbm = pl.BlockSpec(memory_space=pl.ANY)
    dma = pltpu.SemaphoreType.DMA
    args = (
        start_state,
        coefficients,
        w_in,
        w_out.T,
        jacobian.T,
        sigma.reshape(1, channels),
        obs_values,
        owner.T,
        stencil.T,
        counts.reshape(1, rows),
    )
    grad_state, departures, grad_w_in, grad_w_out_t = pl.pallas_call(
        window_kernel,
        out_shape=(
            shape(tlat, feat, width),
            shape(rows, channels),
            shape(feat, hid),
            shape(feat, hid),
        ),
        in_specs=[hbm] + [vmem] * (len(args) - 1),
        out_specs=(hbm, vmem, vmem, vmem),
        scratch_shapes=[field] * 4
        + [
            pltpu.VMEM((tlat, feat, width), f32),
            pltpu.VMEM((4, feat, width), f32),
            pltpu.VMEM((4, feat, width), f32),
            pltpu.VMEM((4, feat, width), f32),
            pltpu.VMEM((feat, width), f32),
            pltpu.VMEM((5, feat, width), f32),
            pltpu.VMEM((2 * width, 2 * width), bf16),
            pltpu.VMEM((tlat // BACK_ROWS, hid, BACK_ROWS * width), f32),
            pltpu.VMEM((tlat // BACK_ROWS, hid, BACK_ROWS * width), f32),
            pltpu.VMEM((hid, feat), bf16),
            pltpu.VMEM((hid, feat), bf16),
            pltpu.VMEM((8, rows), jnp.int32),
            pltpu.VMEM((devices, CAP + META, width), f32),
            pltpu.VMEM((devices, CAP + META, width), f32),
            pltpu.VMEM((META, slots), jnp.int32),
            pltpu.VMEM((tlat // PICK_ROWS if keep else 1, PICK_ROWS * width, slots), bf16),
            pltpu.VMEM((2 * feat, slots), f32),
            pltpu.VMEM((2 * feat, slots), bf16),
            pltpu.VMEM((devices, CAP, channels), f32),
            pltpu.VMEM((devices, CAP, channels), f32),
            pltpu.VMEM((feat, hid), f32),
            pltpu.VMEM((feat, hid), f32),
            pltpu.VMEM((devices, share, width), f32),
            pltpu.VMEM((devices, share, width), f32),
            pltpu.VMEM((share, width), f32),
            pltpu.VMEM((devices, share, width), f32),
            dma((1,)),
            dma((1,)),
            dma((4, 4)),
            dma((4, 4)),
        ]
        + [dma((devices,))] * 8,
        compiler_params=pltpu.CompilerParams(
            collective_id=0, has_side_effects=True, vmem_limit_bytes=VMEM_LIMIT
        ),
    )(*args)
    return grad_state, departures, grad_w_in, grad_w_out_t.T


def solution(mesh):
    return jax.shard_map(
        on_device,
        mesh=mesh,
        in_specs=(
            P("lat", None, "lon"),
            P(),
            P(),
            P(),
            P(),
            P(),
            P(("lat", "lon"), None),
            P(("lat", "lon"), None),
            P(("lat", "lon"), None),
            P(("lat", "lon")),
        ),
        out_specs=(P("lat", None, "lon"), P(("lat", "lon"), None), P(), P()),
        check_vma=False,
    )
```

```python
import functools
import math

import jax
import jax.numpy as jnp
from jax import lax
from jax.experimental import pallas as pl
from jax.experimental.pallas import tpu as pltpu
from jax.sharding import PartitionSpec as P

CAP = 16
CLOSURE_ROWS = 16
BACK_ROWS = 8
PICK_ROWS = 4
PASS_ROWS = 16
COPY_PARTS = 8
SLOT_BLOCK = 512
META = 8
VMEM_LIMIT = 60 * 1024 * 1024
PICK_BYTES = 10 * 1024 * 1024
corner_tenths = (4, 3, 2, 1)
TENTH = 0.1
FORWARD, ADJOINT = (0, 1, 2, 3, 4), (0, 2, 1, 4, 3)
bf16, f32 = jnp.bfloat16, jnp.float32


def mm(a, b):
    return jnp.dot(a, b, preferred_element_type=f32)


def mm_nt(a, b, precision=None):
    return lax.dot_general(
        a, b, (((1,), (1,)), ((), ())), precision=precision, preferred_element_type=f32
    )


def two_parts(x):
    high = x.astype(bf16)
    low = (x - high.astype(f32)).astype(bf16)
    return high, low


def three_parts(x):
    high = x.astype(bf16)
    rest = x - high.astype(f32)
    middle = rest.astype(bf16)
    low = (rest - middle.astype(f32)).astype(bf16)
    return high, middle, low


def turn(x):
    return jnp.transpose(x.astype(f32)).astype(x.dtype)


def picks(local, cells):
    slots = local.shape[1]
    low = local.astype(jnp.int16)
    cell = lax.broadcasted_iota(jnp.int16, (cells, slots), 0)
    zero = jnp.zeros((cells, slots), bf16)
    pick = zero
    for k in range(4):
        same = cell == jnp.broadcast_to(low[k : k + 1], (cells, slots))
        pick = pick + jnp.where(same, jnp.full_like(zero, corner_tenths[k]), zero)
    return pick


def gather_rows(ref, base, count):
    return jnp.concatenate([ref[base + g + 1] for g in range(count)], axis=1).astype(bf16)


def merge_edges(from_west, from_east):
    feat, width = from_west.shape
    lane = lax.broadcasted_iota(jnp.int32, (feat, width), 1)
    return jnp.where(
        lane % 2 == 0, pltpu.roll(from_east, width - 1, axis=1), pltpu.roll(from_west, 1, axis=1)
    )


def edge_pass(field, edge):
    rows, feat, width = field.shape
    pair = lax.broadcasted_iota(jnp.int32, (8, width), 1) >> 1

    def step(b, carry):
        part = pl.ds(pl.multiple_of(b * 8, 8), 8)
        kept = []
        for first in range(0, rows - 2, PASS_ROWS):
            total = jnp.zeros((8, width), f32)
            for i in range(first, first + PASS_ROWS):
                moved = pltpu.roll(field[i + 1, part], 2 * i + 1, axis=1)
                total = jnp.where(pair == i, moved, total)
            kept.append(total)
        edge[part] = sum(kept)
        return carry

    lax.fori_loop(0, feat // 8, step, 0)


def shift_matrix(width):
    row = lax.broadcasted_iota(jnp.int32, (2 * width, 2 * width), 0) % width
    column = lax.broadcasted_iota(jnp.int32, (2 * width, 2 * width), 1)
    taken = jnp.where(column < width, column - 1, column - width + 1)
    return (row == taken).astype(f32).astype(bf16)


def stencil_pass(field, sides, weights, shifts, order, base, out, edge=None, shift=0):
    rows, feat, width = field.shape
    lane = lax.broadcasted_iota(jnp.int32, (8, width), 1)
    pair = lane >> 1

    def step(b, carry):
        part = pl.ds(pl.multiple_of(b * 8, 8), 8)
        centre, north, south, west, east = [weights[k, part] for k in order]
        ends = jnp.where(lane == 0, west, jnp.where(lane == width - 1, east, 0.0))
        side = sides[part]
        inner = field[1 : rows - 1, part].reshape((rows - 2) * 8, width)
        beside = mm(jnp.concatenate(two_parts(inner), axis=1), shifts[...])

        def read(start):
            fresh = range(start, min(start + PASS_ROWS, rows - 2))
            return [field[i + 2, part] for i in fresh], [base[i + shift, part] for i in fresh]

        before, here = field[0, part], field[1, part]
        kept = []
        ready = read(0)
        for start in range(0, rows - 2, PASS_ROWS):
            afters, bases = ready
            ready = read(start + PASS_ROWS)
            results = []
            for i, after, total in zip(range(start, start + PASS_ROWS), afters, bases):
                near = beside[i * 8 : (i + 1) * 8]
                results.append(
                    total
                    + centre * here
                    + north * before
                    + south * after
                    + west * near[:, :width]
                    + east * near[:, width:]
                    + ends * pltpu.roll(side, width - 1 - 2 * i, axis=1)
                )
                before, here = here, after
            for g, row in enumerate(results):
                out[start + g + shift, part] = row
            if edge is not None:
                total = jnp.zeros((8, width), f32)
                for g, row in enumerate(results):
                    i = start + g
                    total = jnp.where(pair == i, pltpu.roll(row, 2 * i + 1, axis=1), total)
                kept.append(total)
        if edge is not None:
            edge[part] = sum(kept)
        return carry

    lax.fori_loop(0, feat // 8, step, 0)


def remote(src, dst, send, recv, to):
    return pltpu.make_async_remote_copy(
        src_ref=src,
        dst_ref=dst,
        send_sem=send,
        recv_sem=recv,
        device_id=to,
        device_id_type=pl.DeviceIdType.MESH,
    )


def window_kernel(
    start_ref,
    coef_ref,
    w_in_ref,
    w_out_t_ref,
    jac_t_ref,
    sigma_ref,
    obs_ref,
    owner_ref,
    stencil_ref,
    counts_ref,
    grad_ref,
    dep_ref,
    gin_out,
    gout_out,
    x0,
    x1,
    a2,
    a1,
    half,
    edges,
    from_west,
    from_east,
    sides,
    weights,
    shifts,
    tanh_0,
    tanh_1,
    w_in_t,
    w_out,
    slot_row,
    obs_send,
    obs_recv,
    cells,
    pick_store,
    acc,
    parts,
    dep_send,
    dep_recv,
    gin,
    gout,
    pair_send,
    pair_recv,
    rs_send,
    rs_recv,
    ag_send,
    ag_recv,
    whole,
    load_sem,
    store_sem,
    halo_send,
    halo_recv,
    obs_ssem,
    obs_rsem,
    dep_ssem,
    dep_rsem,
    pair_ssem,
    pair_rsem,
    rs_ssem,
    rs_rsem,
    ag_ssem,
    ag_rsem,
):
    tlat, feat, width = start_ref.shape
    hid = w_in_ref.shape[1]
    rows, channels = obs_ref.shape
    slots = cells.shape[1]
    block = min(slots, SLOT_BLOCK)
    lat, lon = lax.axis_index("lat"), lax.axis_index("lon")
    lats, lons = lax.axis_size("lat"), lax.axis_size("lon")
    devices = lats * lons
    me = lat * lons + lon
    south, north = {"lat": lax.rem(lat + 1, lats)}, {"lat": lax.rem(lat + lats - 1, lats)}
    east, west = {"lon": lax.rem(lon + 1, lons)}, {"lon": lax.rem(lon + lons - 1, lons)}

    load = pltpu.make_async_copy(start_ref, x0.at[pl.ds(1, tlat)], load_sem.at[0])
    load.start()

    def place(index):
        return {"lat": index // lons, "lon": lax.rem(index, lons)}

    barrier = pltpu.get_barrier_semaphore()

    def greet(k, carry):
        pl.semaphore_signal(
            barrier,
            inc=1,
            device_id=place(lax.rem(me + k, devices)),
            device_id_type=pl.DeviceIdType.MESH,
        )
        return carry

    lax.fori_loop(1, devices, greet, 0)

    def swap(source, target, send, recv, spread=False, own=me, count=devices, place=place):
        def copy_to(k):
            peer = lax.rem(own + k, count)
            return remote(
                source if spread else source.at[peer],
                target.at[own],
                send.at[k],
                recv.at[k],
                place(peer),
            )

        def start():
            def body(k, carry):
                copy_to(k).start()
                return carry

            lax.fori_loop(1, count, body, 0)
            target[own] = source[...] if spread else source[own]

        def finish():
            def body(k, carry):
                copy_to(k).wait()
                return carry

            lax.fori_loop(1, count, body, 0)

        return start, finish

    def halo(number, field):
        sources = (
            (field.at[tlat], field.at[0], south),
            (field.at[1], field.at[tlat + 1], north),
            (edges.at[number], from_west.at[number], east),
            (edges.at[number], from_east.at[number], west),
        )
        copies = [
            remote(src, dst, halo_send.at[number, k], halo_recv.at[number, k], to)
            for k, (src, dst, to) in enumerate(sources)
        ]

        def start():
            for copy in copies:
                copy.start()

        def finish():
            for copy in copies:
                copy.wait()

            @pl.when(lat == 0)
            def _():
                field[0] = jnp.zeros((feat, width), f32)

            @pl.when(lat == lats - 1)
            def _():
                field[tlat + 1] = jnp.zeros((feat, width), f32)

            sides[...] = merge_edges(from_west[number], from_east[number])

        return start, finish

    owner = owner_ref[...]
    tile = lax.broadcasted_iota(jnp.int32, (devices, rows), 0)
    named = (tile == jnp.broadcast_to(owner, (devices, rows))).astype(f32)
    earlier = (
        lax.broadcasted_iota(jnp.int32, (rows, rows), 0)
        < lax.broadcasted_iota(jnp.int32, (rows, rows), 1)
    ).astype(f32)
    before = mm(named.astype(bf16), earlier.astype(bf16))
    rank = jnp.sum(named * before, axis=0, keepdims=True)
    slot = owner * CAP + rank.astype(jnp.int32)
    slot_row[...] = jnp.broadcast_to(slot, slot_row.shape)
    w_in_t[...] = turn(w_in_ref[...])
    w_out[...] = turn(w_out_t_ref[...])

    obs_parts = jnp.concatenate(three_parts(obs_ref[...]), axis=1)
    stencil = stencil_ref[...]
    filler = jnp.zeros((META - 5, rows), f32)
    meta = jnp.concatenate(
        [
            (stencil // width).astype(f32),
            counts_ref[...].astype(f32),
            filler,
            (stencil % width).astype(f32),
            jnp.zeros((META - 4, rows), f32),
        ],
        axis=0,
    ).astype(bf16)
    per_group = width // CAP
    for s in range(0, slots, block):
        here = jnp.broadcast_to(slot, (block, rows)) - s
        pick = (lax.broadcasted_iota(jnp.int32, (block, rows), 0) == here).astype(f32).astype(bf16)
        wide = mm(pick, obs_parts)
        values = wide[:, :channels] + wide[:, channels : 2 * channels] + wide[:, 2 * channels :]
        for t in range(block // CAP):
            obs_send[s // CAP + t, :CAP] = values[t * CAP : (t + 1) * CAP]
        both = mm_nt(meta, pick)
        scale = jnp.where(
            lax.broadcasted_iota(jnp.int32, (META, block), 0) < 4, float(width), 1.0
        )
        lines = both[:META] * scale + both[META:]
        for t in range(block // CAP):
            g = t // per_group
            line = lines[:, g * width : (g + 1) * width]
            shift = (width - (t % per_group) * CAP) % width
            obs_send[s // CAP + t, CAP:] = pltpu.roll(line, shift, axis=1) if shift else line

    load.wait()
    edge_pass(x0, edges.at[0])
    shifts[...] = shift_matrix(width)
    turned = jnp.transpose(coef_ref[...])
    for k in range(5):
        weights[k] = jnp.broadcast_to(turned[:, k : k + 1], (feat, width))

    pl.semaphore_wait(barrier, devices - 1)
    halo_0, halo_1 = halo(0, x0), halo(1, x1)
    halo_2, halo_3 = halo(2, a2), halo(3, a1)
    halo_0[0]()
    obs_start, obs_finish = swap(obs_send, obs_recv, obs_ssem, obs_rsem)
    obs_start()

    per_step = CLOSURE_ROWS // BACK_ROWS

    def closure(field, kept, out, shift):
        def step(b, carry):
            base = b * CLOSURE_ROWS
            inputs = gather_rows(field, base, CLOSURE_ROWS)
            tanh_pre = jnp.tanh(mm(w_in_t[...], inputs))
            for g in range(per_step):
                columns = slice(g * BACK_ROWS * width, (g + 1) * BACK_ROWS * width)
                kept[b * per_step + g] = tanh_pre[:, columns]
            result = mm(w_out_t_ref[...], tanh_pre.astype(bf16))
            for g in range(CLOSURE_ROWS):
                out[base + g + shift] = result[:, g * width : (g + 1) * width]
            return carry

        lax.fori_loop(0, tlat // CLOSURE_ROWS, step, 0)

    closure(x0, tanh_0, x1, 1)
    halo_0[1]()
    stencil_pass(x0, sides, weights, shifts, FORWARD, x1, x1, edges.at[1], 1)
    halo_1[0]()

    closure(x1, tanh_1, half, 0)
    obs_finish()
    lane = lax.broadcasted_iota(jnp.int32, (META, width), 1)
    for g in range(devices // per_group):
        line = obs_recv[g * per_group, CAP:]
        for t in range(1, per_group):
            moved = pltpu.roll(obs_recv[g * per_group + t, CAP:], t * CAP, axis=1)
            line = jnp.where(lane >= t * CAP, moved, line)
        cells[:, g * width : (g + 1) * width] = line.astype(jnp.int32)
    halo_1[1]()
    stencil_pass(x1, sides, weights, shifts, FORWARD, half, half)
    acc[...] = jnp.zeros_like(acc)
    keep = tlat * width * slots * 2 <= PICK_BYTES

    def interpolate(b, carry):
        base = b * PICK_ROWS
        state = jnp.concatenate([half[base + g] for g in range(PICK_ROWS)], axis=1)
        both = jnp.concatenate(two_parts(state), axis=0)
        for s in range(0, slots, block):
            pick = picks(cells[:, s : s + block] - base * width, PICK_ROWS * width)
            if keep:
                pick_store[b, : PICK_ROWS * width, s : s + block] = pick
            acc[:, s : s + block] += mm(both, pick)
        return carry

    lax.fori_loop(0, tlat // PICK_ROWS, interpolate, 0)

    jac_t = jac_t_ref[...]
    sigma = sigma_ref[...]
    for s in range(0, slots, block):
        interp = jnp.transpose((acc[:feat, s : s + block] + acc[feat:, s : s + block]) * TENTH)
        evolved = jnp.dot(
            interp, jac_t, precision=lax.Precision.HIGHEST, preferred_element_type=f32
        )
        counts = jnp.transpose(cells[:, s : s + block].astype(f32))[:, 4:5]
        channel = lax.broadcasted_iota(jnp.int32, (block, channels), 1).astype(f32)
        used = channel < jnp.broadcast_to(counts, (block, channels))
        obs = obs_recv[s // CAP : (s + block) // CAP, :CAP].reshape(block, channels)
        departures = jnp.where(used, (obs - evolved) / sigma, 0.0)
        dep_send[s // CAP : (s + block) // CAP] = departures.reshape(block // CAP, CAP, channels)
        pulled = mm_nt(jac_t, -departures / sigma, lax.Precision.HIGHEST)
        parts[:, s : s + block] = jnp.concatenate(two_parts(pulled * TENTH), axis=0)
    dep_start, dep_finish = swap(dep_send, dep_recv, dep_ssem, dep_rsem)
    dep_start()

    def spread(b, carry):
        base = b * PICK_ROWS
        total = jnp.zeros((2 * feat, PICK_ROWS * width), f32)
        for s in range(0, slots, block):
            if keep:
                pick = pick_store[b, : PICK_ROWS * width, s : s + block]
            else:
                pick = picks(cells[:, s : s + block] - base * width, PICK_ROWS * width)
            total = total + mm_nt(parts[:, s : s + block], pick)
        out = total[:feat] + total[feat:]
        for g in range(PICK_ROWS):
            a2[base + g + 1] = out[:, g * width : (g + 1) * width]
        return carry

    lax.fori_loop(0, tlat // PICK_ROWS, spread, 0)
    edge_pass(a2, edges.at[2])
    halo_2[0]()

    gin[...] = jnp.zeros_like(gin)
    gout[...] = jnp.zeros_like(gout)

    def closure_back(state, kept, cot_field, out, shift):
        def step(b, carry):
            base = b * BACK_ROWS
            inputs = gather_rows(state, base, BACK_ROWS)
            cot = gather_rows(cot_field, base, BACK_ROWS)
            tanh_pre = kept[b]
            gout[...] += mm_nt(cot, tanh_pre.astype(bf16))
            back_hidden = mm(w_out[...], cot)
            back_pre = (back_hidden * (1.0 - tanh_pre * tanh_pre)).astype(bf16)
            gin[...] += mm_nt(inputs, back_pre)
            back = mm(w_in_ref[...], back_pre)
            for g in range(BACK_ROWS):
                out[base + g + shift] = back[:, g * width : (g + 1) * width]
            return carry

        lax.fori_loop(0, tlat // BACK_ROWS, step, 0)

    closure_back(x1, tanh_1, a2, a1, 1)
    halo_2[1]()
    stencil_pass(a2, sides, weights, shifts, ADJOINT, a1, a1, edges.at[3], 1)
    halo_3[0]()

    side = lax.rem(lat, 2)
    partner = {"lat": lat + 1 - 2 * side}
    pairs = devices // 2
    pair = (lat // 2) * lons + lon
    scale = 1.0 / math.sqrt(tlat * lats * width * lons)
    groups = tlat // BACK_ROWS
    per_group_picks = BACK_ROWS // PICK_ROWS
    span = PICK_ROWS * width
    depth = hid // 2

    def pair_place(index):
        return {"lat": (index // lons) * 2 + side, "lon": lax.rem(index, lons)}

    def half_sum(c):
        first = remote(
            pair_send.at[c, 1 - side],
            pair_recv.at[c],
            pair_ssem.at[c, 0],
            pair_rsem.at[c, 0],
            partner,
        )
        last = remote(
            whole.at[c, side],
            whole.at[c, side],
            pair_ssem.at[c, 1],
            pair_rsem.at[c, 1],
            partner,
        )
        group = dict(own=pair, count=pairs, place=pair_place)
        scatter = swap(rs_send.at[c], rs_recv.at[c], rs_ssem.at[c], rs_rsem.at[c], **group)
        gather = swap(
            ag_send.at[c], ag_recv.at[c], ag_ssem.at[c], ag_rsem.at[c], spread=True, **group
        )

        def begin():
            columns = slice(c * depth, (c + 1) * depth)
            grads = jnp.concatenate([gin[:, columns], gout[:, columns]], axis=0)
            stacked = jnp.concatenate(
                [grads[:, k : k + width] for k in range(0, depth, width)], axis=0
            )
            pair_send[c] = stacked.reshape(pair_send.shape[1:])
            first.start()

        def reduce():
            first.wait()
            rs_send[c] = (pair_send[c, side] + pair_recv[c]).reshape(rs_send.shape[1:])
            scatter[0]()

        def share():
            scatter[1]()
            ag_send[c] = jnp.sum(rs_recv[c], axis=0) * scale
            gather[0]()

        def exchange():
            gather[1]()
            whole[c, side] = ag_recv[c].reshape(whole.shape[2:])
            last.start()

        def end():
            last.wait()
            tiles = whole[c].reshape(depth // width, 2 * feat, width)
            for k in range(depth // width):
                columns = slice(c * depth + k * width, c * depth + (k + 1) * width)
                gin_out[:, columns] = tiles[k, :feat]
                gout_out[:, columns] = tiles[k, feat:]

        return begin, reduce, share, exchange, end

    def half_back(c, first, last):
        units = slice(c * depth, (c + 1) * depth)

        def step(b, carry):
            base = b * BACK_ROWS
            inputs = gather_rows(x0, base, BACK_ROWS)
            cot = gather_rows(a1, base, BACK_ROWS)
            tanh_pre = tanh_0[b, units]
            gout[:, units] += mm_nt(cot, tanh_pre.astype(bf16))
            back_hidden = mm(w_out[units], cot)
            back_pre = (back_hidden * (1.0 - tanh_pre * tanh_pre)).astype(bf16)
            gin[:, units] += mm_nt(inputs, back_pre)
            if keep:
                for k in range(per_group_picks):
                    pick_store[b * per_group_picks + k, units, :span] = back_pre[
                        :, k * span : (k + 1) * span
                    ]
            else:
                tanh_1[b, units] = back_pre.astype(f32)
            return carry

        lax.fori_loop(first, last, step, 0)

    def state_back(first, last):
        def step(b, carry):
            if keep:
                back_pre = jnp.concatenate(
                    [
                        pick_store[b * per_group_picks + k, :hid, :span]
                        for k in range(per_group_picks)
                    ],
                    axis=1,
                )
            else:
                back_pre = tanh_1[b].astype(bf16)
            back = mm(w_in_ref[...], back_pre)
            for g in range(BACK_ROWS):
                half[b * BACK_ROWS + g] = back[:, g * width : (g + 1) * width]
            return carry

        lax.fori_loop(first, last, step, 0)

    sum_0, sum_1 = half_sum(0), half_sum(1)
    half_back(0, 0, groups)
    sum_0[0]()
    half_back(1, 0, groups // 2)
    sum_0[1]()
    half_back(1, groups // 2, groups)
    sum_1[0]()
    dep_finish()
    slot_column = jnp.transpose(slot_row[...].astype(f32))[:, :1].astype(jnp.int32)
    total = jnp.zeros((rows, 3 * channels), f32)
    for s in range(0, slots, block):
        here = jnp.broadcast_to(slot_column, (rows, block)) - s
        pick = (lax.broadcasted_iota(jnp.int32, (rows, block), 1) == here).astype(f32).astype(bf16)
        values = dep_recv[s // CAP : (s + block) // CAP].reshape(block, channels)
        total = total + mm(pick, jnp.concatenate(three_parts(values), axis=1))
    dep_ref[...] = (
        total[:, :channels] + total[:, channels : 2 * channels] + total[:, 2 * channels :]
    )
    sum_0[2]()
    sum_1[1]()
    state_back(0, groups)
    sum_0[3]()
    sum_1[2]()
    halo_3[1]()
    stencil_pass(a1, sides, weights, shifts, ADJOINT, half, half)
    store = pltpu.make_async_copy(half, grad_ref, store_sem.at[0])
    store.start()
    sum_0[4]()
    sum_1[3]()
    sum_1[4]()
    store.wait()


def copy_out_kernel(count, *refs):
    sources, targets, kept = refs[:count], refs[count : 2 * count], refs[2 * count : 3 * count]
    in_sems, out_sems = refs[3 * count :]
    pieces = []
    for source, target, held in zip(sources, targets, kept):
        parts = COPY_PARTS if len(source.shape) == 3 else 1
        size = source.shape[0] // parts
        for k in range(parts):
            part = pl.ds(k * size, size)
            pieces.append((source.at[part], held.at[part], target.at[part]))
    loads = [
        pltpu.make_async_copy(source, held, in_sems.at[n])
        for n, (source, held, _) in enumerate(pieces)
    ]
    stores = [
        pltpu.make_async_copy(held, target, out_sems.at[n])
        for n, (_, held, target) in enumerate(pieces)
    ]
    for load in loads:
        load.start()
    for load, store in zip(loads, stores):
        load.wait()
        store.start()
    for store in stores:
        store.wait()


def copy_out(*arrays):
    hbm = pl.BlockSpec(memory_space=pl.ANY)
    count = len(arrays)
    sems = pltpu.SemaphoreType.DMA((COPY_PARTS + count - 1,))
    return pl.pallas_call(
        functools.partial(copy_out_kernel, count),
        out_shape=tuple(jax.ShapeDtypeStruct(a.shape, a.dtype) for a in arrays),
        in_specs=[hbm] * count,
        out_specs=(hbm,) * count,
        scratch_shapes=[pltpu.VMEM(a.shape, a.dtype) for a in arrays] + [sems, sems],
    )(*arrays)


def on_device(
    start_state, coefficients, w_in, w_out, jacobian, sigma, obs_values, owner, stencil, counts
):
    tlat, feat, width = start_state.shape
    rows, channels = obs_values.shape
    hid = w_in.shape[1]
    devices = lax.axis_size("lat") * lax.axis_size("lon")
    slots = devices * CAP
    cell_count = tlat * width
    assert cell_count <= 1 << 15 and 2 * tlat <= width and max(width, channels) <= 256
    side_rows = hid * feat // (2 * width)
    share = side_rows // (devices // 2)
    assert side_rows % (devices // 2) == 0 and width % CAP == 0
    assert channels == width and hid % (2 * width) == 0 and lax.axis_size("lat") % 2 == 0
    span = PICK_ROWS * width
    keep = cell_count * slots * 2 <= PICK_BYTES
    store_shape = (
        (tlat // PICK_ROWS, max(hid, span), max(slots, span))
        if keep
        else (1, 16, width)
    )
    field = pltpu.VMEM((tlat + 2, feat, width), f32)
    shape = lambda *dims: jax.ShapeDtypeStruct(dims, f32)
    vmem = pl.BlockSpec(memory_space=pltpu.VMEM)
    hbm = pl.BlockSpec(memory_space=pl.ANY)
    dma = pltpu.SemaphoreType.DMA
    args = (
        start_state,
        coefficients,
        w_in,
        w_out.T,
        jacobian.T,
        sigma.reshape(1, channels),
        obs_values,
        owner.T,
        stencil.T,
        counts.reshape(1, rows),
    )
    grad_state, departures, grad_w_in, grad_w_out_t = pl.pallas_call(
        window_kernel,
        out_shape=(
            shape(tlat, feat, width),
            shape(rows, channels),
            shape(feat, hid),
            shape(feat, hid),
        ),
        in_specs=[hbm] + [vmem] * (len(args) - 1),
        out_specs=(hbm, vmem, vmem, vmem),
        scratch_shapes=[field] * 4
        + [
            pltpu.VMEM((tlat, feat, width), f32),
            pltpu.VMEM((4, feat, width), f32),
            pltpu.VMEM((4, feat, width), f32),
            pltpu.VMEM((4, feat, width), f32),
            pltpu.VMEM((feat, width), f32),
            pltpu.VMEM((5, feat, width), f32),
            pltpu.VMEM((2 * width, 2 * width), bf16),
            pltpu.VMEM((tlat // BACK_ROWS, hid, BACK_ROWS * width), f32),
            pltpu.VMEM((tlat // BACK_ROWS, hid, BACK_ROWS * width), f32),
            pltpu.VMEM((hid, feat), bf16),
            pltpu.VMEM((hid, feat), bf16),
            pltpu.VMEM((8, rows), jnp.int32),
            pltpu.VMEM((devices, CAP + META, width), f32),
            pltpu.VMEM((devices, CAP + META, width), f32),
            pltpu.VMEM((META, slots), jnp.int32),
            pltpu.VMEM(store_shape, bf16),
            pltpu.VMEM((2 * feat, slots), f32),
            pltpu.VMEM((2 * feat, slots), bf16),
            pltpu.VMEM((devices, CAP, channels), f32),
            pltpu.VMEM((devices, CAP, channels), f32),
            pltpu.VMEM((feat, hid), f32),
            pltpu.VMEM((feat, hid), f32),
            pltpu.VMEM((2, 2, side_rows, width), f32),
            pltpu.VMEM((2, side_rows, width), f32),
            pltpu.VMEM((2, devices // 2, share, width), f32),
            pltpu.VMEM((2, devices // 2, share, width), f32),
            pltpu.VMEM((2, share, width), f32),
            pltpu.VMEM((2, devices // 2, share, width), f32),
            pltpu.VMEM((2, 2, side_rows, width), f32),
            dma((1,)),
            dma((1,)),
            dma((4, 4)),
            dma((4, 4)),
        ]
        + [dma((devices,))] * 4
        + [dma((2, 2))] * 2
        + [dma((2, devices // 2))] * 4,
        compiler_params=pltpu.CompilerParams(
            collective_id=0, has_side_effects=True, vmem_limit_bytes=VMEM_LIMIT
        ),
    )(*args)
    grad_state, departures, grad_w_in, grad_w_out_t = copy_out(
        grad_state, departures, grad_w_in, grad_w_out_t
    )
    return grad_state, departures, grad_w_in, grad_w_out_t.T


def solution(mesh):
    return jax.shard_map(
        on_device,
        mesh=mesh,
        in_specs=(
            P("lat", None, "lon"),
            P(),
            P(),
            P(),
            P(),
            P(),
            P(("lat", "lon"), None),
            P(("lat", "lon"), None),
            P(("lat", "lon"), None),
            P(("lat", "lon")),
        ),
        out_specs=(P("lat", None, "lon"), P(("lat", "lon"), None), P(), P()),
        check_vma=False,
    )
```

```python
import functools
import math

import jax
import jax.numpy as jnp
from jax import lax
from jax.experimental import pallas as pl
from jax.experimental.pallas import tpu as pltpu
from jax.sharding import PartitionSpec as P

CAP = 16
CLOSURE_ROWS = 16
BACK_ROWS = 8
PICK_ROWS = 4
PASS_ROWS = 16
COPY_PARTS = 8
BACK_UNROLL, PICK_UNROLL, PASS_UNROLL, CLOSURE_UNROLL = 4, 4, 4, 1
SLOT_BLOCK = 512
META = 8
VMEM_LIMIT = 60 * 1024 * 1024
PICK_BYTES = 10 * 1024 * 1024
corner_tenths = (4, 3, 2, 1)
TENTH = 0.1
FORWARD, ADJOINT = (0, 1, 2, 3, 4), (0, 2, 1, 4, 3)
bf16, f32 = jnp.bfloat16, jnp.float32


def mm(a, b):
    return jnp.dot(a, b, preferred_element_type=f32)


def mm_nt(a, b, precision=None):
    return lax.dot_general(
        a, b, (((1,), (1,)), ((), ())), precision=precision, preferred_element_type=f32
    )


def two_parts(x):
    high = x.astype(bf16)
    low = (x - high.astype(f32)).astype(bf16)
    return high, low


def three_parts(x):
    high = x.astype(bf16)
    rest = x - high.astype(f32)
    middle = rest.astype(bf16)
    low = (rest - middle.astype(f32)).astype(bf16)
    return high, middle, low


def turn(x):
    return jnp.transpose(x.astype(f32)).astype(x.dtype)


def picks(local, cells):
    slots = local.shape[1]
    low = local.astype(jnp.int16)
    cell = lax.broadcasted_iota(jnp.int16, (cells, slots), 0)
    zero = jnp.zeros((cells, slots), bf16)
    pick = zero
    for k in range(4):
        same = cell == jnp.broadcast_to(low[k : k + 1], (cells, slots))
        pick = pick + jnp.where(same, jnp.full_like(zero, corner_tenths[k]), zero)
    return pick


def gather_rows(ref, base, count):
    return jnp.concatenate([ref[base + g + 1] for g in range(count)], axis=1).astype(bf16)


def merge_edges(from_west, from_east):
    feat, width = from_west.shape
    lane = lax.broadcasted_iota(jnp.int32, (feat, width), 1)
    return jnp.where(
        lane % 2 == 0, pltpu.roll(from_east, width - 1, axis=1), pltpu.roll(from_west, 1, axis=1)
    )


def edge_pass(field, edge):
    rows, feat, width = field.shape
    pair = lax.broadcasted_iota(jnp.int32, (8, width), 1) >> 1

    def step(b, carry):
        part = pl.ds(pl.multiple_of(b * 8, 8), 8)
        kept = []
        for first in range(0, rows - 2, PASS_ROWS):
            total = jnp.zeros((8, width), f32)
            for i in range(first, first + PASS_ROWS):
                moved = pltpu.roll(field[i + 1, part], 2 * i + 1, axis=1)
                total = jnp.where(pair == i, moved, total)
            kept.append(total)
        edge[part] = sum(kept)
        return carry

    lax.fori_loop(0, feat // 8, step, 0, unroll=PASS_UNROLL)


def shift_matrix(width):
    row = lax.broadcasted_iota(jnp.int32, (2 * width, 2 * width), 0) % width
    column = lax.broadcasted_iota(jnp.int32, (2 * width, 2 * width), 1)
    taken = jnp.where(column < width, column - 1, column - width + 1)
    return (row == taken).astype(f32).astype(bf16)


def stencil_pass(field, sides, weights, shifts, order, base, out, edge=None, shift=0):
    rows, feat, width = field.shape
    lane = lax.broadcasted_iota(jnp.int32, (8, width), 1)
    pair = lane >> 1

    def step(b, carry):
        part = pl.ds(pl.multiple_of(b * 8, 8), 8)
        centre, north, south, west, east = [weights[k, part] for k in order]
        ends = jnp.where(lane == 0, west, jnp.where(lane == width - 1, east, 0.0))
        side = sides[part]
        inner = field[1 : rows - 1, part].reshape((rows - 2) * 8, width)
        beside = mm(jnp.concatenate(two_parts(inner), axis=1), shifts[...])

        def read(start):
            fresh = range(start, min(start + PASS_ROWS, rows - 2))
            return [field[i + 2, part] for i in fresh], [base[i + shift, part] for i in fresh]

        before, here = field[0, part], field[1, part]
        kept = []
        ready = read(0)
        for start in range(0, rows - 2, PASS_ROWS):
            afters, bases = ready
            ready = read(start + PASS_ROWS)
            results = []
            for i, after, total in zip(range(start, start + PASS_ROWS), afters, bases):
                near = beside[i * 8 : (i + 1) * 8]
                results.append(
                    total
                    + centre * here
                    + north * before
                    + south * after
                    + west * near[:, :width]
                    + east * near[:, width:]
                    + ends * pltpu.roll(side, width - 1 - 2 * i, axis=1)
                )
                before, here = here, after
            for g, row in enumerate(results):
                out[start + g + shift, part] = row
            if edge is not None:
                total = jnp.zeros((8, width), f32)
                for g, row in enumerate(results):
                    i = start + g
                    total = jnp.where(pair == i, pltpu.roll(row, 2 * i + 1, axis=1), total)
                kept.append(total)
        if edge is not None:
            edge[part] = sum(kept)
        return carry

    lax.fori_loop(0, feat // 8, step, 0, unroll=PASS_UNROLL)


def remote(src, dst, send, recv, to):
    return pltpu.make_async_remote_copy(
        src_ref=src,
        dst_ref=dst,
        send_sem=send,
        recv_sem=recv,
        device_id=to,
        device_id_type=pl.DeviceIdType.MESH,
    )


def window_kernel(
    start_ref,
    coef_ref,
    w_in_ref,
    w_out_t_ref,
    jac_t_ref,
    sigma_ref,
    obs_ref,
    owner_ref,
    stencil_ref,
    counts_ref,
    grad_ref,
    dep_ref,
    gin_out,
    gout_out,
    x0,
    x1,
    a2,
    a1,
    half,
    edges,
    from_west,
    from_east,
    sides,
    weights,
    shifts,
    tanh_0,
    tanh_1,
    w_in_t,
    w_out,
    slot_row,
    obs_send,
    obs_recv,
    cells,
    pick_store,
    acc,
    parts,
    dep_send,
    dep_recv,
    gin,
    gout,
    pair_send,
    pair_recv,
    rs_send,
    rs_recv,
    ag_send,
    ag_recv,
    whole,
    load_sem,
    store_sem,
    halo_send,
    halo_recv,
    obs_ssem,
    obs_rsem,
    dep_ssem,
    dep_rsem,
    pair_ssem,
    pair_rsem,
    rs_ssem,
    rs_rsem,
    ag_ssem,
    ag_rsem,
):
    tlat, feat, width = start_ref.shape
    hid = w_in_ref.shape[1]
    rows, channels = obs_ref.shape
    slots = cells.shape[1]
    block = min(slots, SLOT_BLOCK)
    lat, lon = lax.axis_index("lat"), lax.axis_index("lon")
    lats, lons = lax.axis_size("lat"), lax.axis_size("lon")
    devices = lats * lons
    me = lat * lons + lon
    south, north = {"lat": lax.rem(lat + 1, lats)}, {"lat": lax.rem(lat + lats - 1, lats)}
    east, west = {"lon": lax.rem(lon + 1, lons)}, {"lon": lax.rem(lon + lons - 1, lons)}

    load = pltpu.make_async_copy(start_ref, x0.at[pl.ds(1, tlat)], load_sem.at[0])
    load.start()

    def place(index):
        return {"lat": index // lons, "lon": lax.rem(index, lons)}

    barrier = pltpu.get_barrier_semaphore()

    def greet(k, carry):
        pl.semaphore_signal(
            barrier,
            inc=1,
            device_id=place(lax.rem(me + k, devices)),
            device_id_type=pl.DeviceIdType.MESH,
        )
        return carry

    lax.fori_loop(1, devices, greet, 0)

    def swap(source, target, send, recv, spread=False, own=me, count=devices, place=place):
        def copy_to(k):
            peer = lax.rem(own + k, count)
            return remote(
                source if spread else source.at[peer],
                target.at[own],
                send.at[k],
                recv.at[k],
                place(peer),
            )

        def start():
            def body(k, carry):
                copy_to(k).start()
                return carry

            lax.fori_loop(1, count, body, 0)
            target[own] = source[...] if spread else source[own]

        def finish():
            def body(k, carry):
                copy_to(k).wait()
                return carry

            lax.fori_loop(1, count, body, 0)

        return start, finish

    def halo(number, field):
        sources = (
            (field.at[tlat], field.at[0], south),
            (field.at[1], field.at[tlat + 1], north),
            (edges.at[number], from_west.at[number], east),
            (edges.at[number], from_east.at[number], west),
        )
        copies = [
            remote(src, dst, halo_send.at[number, k], halo_recv.at[number, k], to)
            for k, (src, dst, to) in enumerate(sources)
        ]

        def start():
            for copy in copies:
                copy.start()

        def finish():
            for copy in copies:
                copy.wait()

            @pl.when(lat == 0)
            def _():
                field[0] = jnp.zeros((feat, width), f32)

            @pl.when(lat == lats - 1)
            def _():
                field[tlat + 1] = jnp.zeros((feat, width), f32)

            sides[...] = merge_edges(from_west[number], from_east[number])

        return start, finish

    owner = owner_ref[...]
    tile = lax.broadcasted_iota(jnp.int32, (devices, rows), 0)
    named = (tile == jnp.broadcast_to(owner, (devices, rows))).astype(f32)
    earlier = (
        lax.broadcasted_iota(jnp.int32, (rows, rows), 0)
        < lax.broadcasted_iota(jnp.int32, (rows, rows), 1)
    ).astype(f32)
    before = mm(named.astype(bf16), earlier.astype(bf16))
    rank = jnp.sum(named * before, axis=0, keepdims=True)
    slot = owner * CAP + rank.astype(jnp.int32)
    slot_row[...] = jnp.broadcast_to(slot, slot_row.shape)
    w_in_t[...] = turn(w_in_ref[...])
    w_out[...] = turn(w_out_t_ref[...])

    obs_parts = jnp.concatenate(three_parts(obs_ref[...]), axis=1)
    stencil = stencil_ref[...]
    filler = jnp.zeros((META - 5, rows), f32)
    meta = jnp.concatenate(
        [
            (stencil // width).astype(f32),
            counts_ref[...].astype(f32),
            filler,
            (stencil % width).astype(f32),
            jnp.zeros((META - 4, rows), f32),
        ],
        axis=0,
    ).astype(bf16)
    per_group = width // CAP
    for s in range(0, slots, block):
        here = jnp.broadcast_to(slot, (block, rows)) - s
        pick = (lax.broadcasted_iota(jnp.int32, (block, rows), 0) == here).astype(f32).astype(bf16)
        wide = mm(pick, obs_parts)
        values = wide[:, :channels] + wide[:, channels : 2 * channels] + wide[:, 2 * channels :]
        for t in range(block // CAP):
            obs_send[s // CAP + t, :CAP] = values[t * CAP : (t + 1) * CAP]
        both = mm_nt(meta, pick)
        scale = jnp.where(
            lax.broadcasted_iota(jnp.int32, (META, block), 0) < 4, float(width), 1.0
        )
        lines = both[:META] * scale + both[META:]
        for t in range(block // CAP):
            g = t // per_group
            line = lines[:, g * width : (g + 1) * width]
            shift = (width - (t % per_group) * CAP) % width
            obs_send[s // CAP + t, CAP:] = pltpu.roll(line, shift, axis=1) if shift else line

    load.wait()
    edge_pass(x0, edges.at[0])
    shifts[...] = shift_matrix(width)
    turned = jnp.transpose(coef_ref[...])
    for k in range(5):
        weights[k] = jnp.broadcast_to(turned[:, k : k + 1], (feat, width))

    pl.semaphore_wait(barrier, devices - 1)
    halo_0, halo_1 = halo(0, x0), halo(1, x1)
    halo_2, halo_3 = halo(2, a2), halo(3, a1)
    halo_0[0]()
    obs_start, obs_finish = swap(obs_send, obs_recv, obs_ssem, obs_rsem)
    obs_start()

    per_step = CLOSURE_ROWS // BACK_ROWS

    def closure(field, kept, out, shift):
        def step(b, carry):
            base = b * CLOSURE_ROWS
            inputs = gather_rows(field, base, CLOSURE_ROWS)
            tanh_pre = jnp.tanh(mm(w_in_t[...], inputs))
            for g in range(per_step):
                columns = slice(g * BACK_ROWS * width, (g + 1) * BACK_ROWS * width)
                kept[b * per_step + g] = tanh_pre[:, columns]
            result = mm(w_out_t_ref[...], tanh_pre.astype(bf16))
            for g in range(CLOSURE_ROWS):
                out[base + g + shift] = result[:, g * width : (g + 1) * width]
            return carry

        lax.fori_loop(0, tlat // CLOSURE_ROWS, step, 0, unroll=CLOSURE_UNROLL)

    closure(x0, tanh_0, x1, 1)
    halo_0[1]()
    stencil_pass(x0, sides, weights, shifts, FORWARD, x1, x1, edges.at[1], 1)
    halo_1[0]()

    closure(x1, tanh_1, half, 0)
    halo_1[1]()
    stencil_pass(x1, sides, weights, shifts, FORWARD, half, half)
    obs_finish()
    lane = lax.broadcasted_iota(jnp.int32, (META, width), 1)
    for g in range(devices // per_group):
        line = obs_recv[g * per_group, CAP:]
        for t in range(1, per_group):
            moved = pltpu.roll(obs_recv[g * per_group + t, CAP:], t * CAP, axis=1)
            line = jnp.where(lane >= t * CAP, moved, line)
        cells[:, g * width : (g + 1) * width] = line.astype(jnp.int32)
    acc[...] = jnp.zeros_like(acc)
    keep = tlat * width * slots * 2 <= PICK_BYTES

    def interpolate(b, carry):
        base = b * PICK_ROWS
        state = jnp.concatenate([half[base + g] for g in range(PICK_ROWS)], axis=1)
        both = jnp.concatenate(two_parts(state), axis=0)
        for s in range(0, slots, block):
            pick = picks(cells[:, s : s + block] - base * width, PICK_ROWS * width)
            if keep:
                pick_store[b, : PICK_ROWS * width, s : s + block] = pick
            acc[:, s : s + block] += mm(both, pick)
        return carry

    lax.fori_loop(0, tlat // PICK_ROWS, interpolate, 0, unroll=PICK_UNROLL)

    jac_t = jac_t_ref[...]
    sigma = sigma_ref[...]
    for s in range(0, slots, block):
        interp = jnp.transpose((acc[:feat, s : s + block] + acc[feat:, s : s + block]) * TENTH)
        evolved = jnp.dot(
            interp, jac_t, precision=lax.Precision.HIGHEST, preferred_element_type=f32
        )
        counts = jnp.transpose(cells[:, s : s + block].astype(f32))[:, 4:5]
        channel = lax.broadcasted_iota(jnp.int32, (block, channels), 1).astype(f32)
        used = channel < jnp.broadcast_to(counts, (block, channels))
        obs = obs_recv[s // CAP : (s + block) // CAP, :CAP].reshape(block, channels)
        departures = jnp.where(used, (obs - evolved) / sigma, 0.0)
        dep_send[s // CAP : (s + block) // CAP] = departures.reshape(block // CAP, CAP, channels)
        pulled = mm_nt(jac_t, -departures / sigma, lax.Precision.HIGHEST)
        parts[:, s : s + block] = jnp.concatenate(two_parts(pulled * TENTH), axis=0)
    dep_start, dep_finish = swap(dep_send, dep_recv, dep_ssem, dep_rsem)
    dep_start()

    def spread(b, carry):
        base = b * PICK_ROWS
        total = jnp.zeros((2 * feat, PICK_ROWS * width), f32)
        for s in range(0, slots, block):
            if keep:
                pick = pick_store[b, : PICK_ROWS * width, s : s + block]
            else:
                pick = picks(cells[:, s : s + block] - base * width, PICK_ROWS * width)
            total = total + mm_nt(parts[:, s : s + block], pick)
        out = total[:feat] + total[feat:]
        for g in range(PICK_ROWS):
            a2[base + g + 1] = out[:, g * width : (g + 1) * width]
        return carry

    lax.fori_loop(0, tlat // PICK_ROWS, spread, 0, unroll=PICK_UNROLL)
    edge_pass(a2, edges.at[2])
    halo_2[0]()

    gin[...] = jnp.zeros_like(gin)
    gout[...] = jnp.zeros_like(gout)

    def closure_back(state, kept, cot_field, out, shift):
        def step(b, carry):
            base = b * BACK_ROWS
            inputs = gather_rows(state, base, BACK_ROWS)
            cot = gather_rows(cot_field, base, BACK_ROWS)
            tanh_pre = kept[b]
            gout[...] += mm_nt(cot, tanh_pre.astype(bf16))
            back_hidden = mm(w_out[...], cot)
            back_pre = (back_hidden * (1.0 - tanh_pre * tanh_pre)).astype(bf16)
            gin[...] += mm_nt(inputs, back_pre)
            back = mm(w_in_ref[...], back_pre)
            for g in range(BACK_ROWS):
                out[base + g + shift] = back[:, g * width : (g + 1) * width]
            return carry

        lax.fori_loop(0, tlat // BACK_ROWS, step, 0, unroll=BACK_UNROLL)

    closure_back(x1, tanh_1, a2, a1, 1)
    halo_2[1]()
    stencil_pass(a2, sides, weights, shifts, ADJOINT, a1, a1, edges.at[3], 1)
    halo_3[0]()

    side = lax.rem(lat, 2)
    partner = {"lat": lat + 1 - 2 * side}
    pairs = devices // 2
    pair = (lat // 2) * lons + lon
    scale = 1.0 / math.sqrt(tlat * lats * width * lons)
    groups = tlat // BACK_ROWS
    per_group_picks = BACK_ROWS // PICK_ROWS
    span = PICK_ROWS * width
    depth = hid // 2

    def pair_place(index):
        return {"lat": (index // lons) * 2 + side, "lon": lax.rem(index, lons)}

    def half_sum(c):
        first = remote(
            pair_send.at[c, 1 - side],
            pair_recv.at[c],
            pair_ssem.at[c, 0],
            pair_rsem.at[c, 0],
            partner,
        )
        last = remote(
            whole.at[c, side],
            whole.at[c, side],
            pair_ssem.at[c, 1],
            pair_rsem.at[c, 1],
            partner,
        )
        group = dict(own=pair, count=pairs, place=pair_place)
        scatter = swap(rs_send.at[c], rs_recv.at[c], rs_ssem.at[c], rs_rsem.at[c], **group)
        gather = swap(
            ag_send.at[c], ag_recv.at[c], ag_ssem.at[c], ag_rsem.at[c], spread=True, **group
        )

        def begin():
            columns = slice(c * depth, (c + 1) * depth)
            grads = jnp.concatenate([gin[:, columns], gout[:, columns]], axis=0)
            stacked = jnp.concatenate(
                [grads[:, k : k + width] for k in range(0, depth, width)], axis=0
            )
            pair_send[c] = stacked.reshape(pair_send.shape[1:])
            first.start()

        def reduce():
            first.wait()
            rs_send[c] = (pair_send[c, side] + pair_recv[c]).reshape(rs_send.shape[1:])
            scatter[0]()

        def share():
            scatter[1]()
            ag_send[c] = jnp.sum(rs_recv[c], axis=0) * scale
            gather[0]()

        def exchange():
            gather[1]()
            whole[c, side] = ag_recv[c].reshape(whole.shape[2:])
            last.start()

        def end():
            last.wait()
            tiles = whole[c].reshape(depth // width, 2 * feat, width)
            for k in range(depth // width):
                columns = slice(c * depth + k * width, c * depth + (k + 1) * width)
                gin_out[:, columns] = tiles[k, :feat]
                gout_out[:, columns] = tiles[k, feat:]

        return begin, reduce, share, exchange, end

    def half_back(c, first, last):
        units = slice(c * depth, (c + 1) * depth)

        def step(b, carry):
            base = b * BACK_ROWS
            inputs = gather_rows(x0, base, BACK_ROWS)
            cot = gather_rows(a1, base, BACK_ROWS)
            tanh_pre = tanh_0[b, units]
            gout[:, units] += mm_nt(cot, tanh_pre.astype(bf16))
            back_hidden = mm(w_out[units], cot)
            back_pre = (back_hidden * (1.0 - tanh_pre * tanh_pre)).astype(bf16)
            gin[:, units] += mm_nt(inputs, back_pre)
            if keep:
                for k in range(per_group_picks):
                    pick_store[b * per_group_picks + k, units, :span] = back_pre[
                        :, k * span : (k + 1) * span
                    ]
            else:
                tanh_1[b, units] = back_pre.astype(f32)
            return carry

        lax.fori_loop(first, last, step, 0, unroll=BACK_UNROLL)

    def state_back(first, last):
        def step(b, carry):
            if keep:
                back_pre = jnp.concatenate(
                    [
                        pick_store[b * per_group_picks + k, :hid, :span]
                        for k in range(per_group_picks)
                    ],
                    axis=1,
                )
            else:
                back_pre = tanh_1[b].astype(bf16)
            back = mm(w_in_ref[...], back_pre)
            for g in range(BACK_ROWS):
                half[b * BACK_ROWS + g] = back[:, g * width : (g + 1) * width]
            return carry

        lax.fori_loop(first, last, step, 0, unroll=BACK_UNROLL)

    sum_0, sum_1 = half_sum(0), half_sum(1)
    half_back(0, 0, groups)
    sum_0[0]()
    half_back(1, 0, groups // 2)
    sum_0[1]()
    half_back(1, groups // 2, groups)
    sum_1[0]()
    dep_finish()
    slot_column = jnp.transpose(slot_row[...].astype(f32))[:, :1].astype(jnp.int32)
    total = jnp.zeros((rows, 3 * channels), f32)
    for s in range(0, slots, block):
        here = jnp.broadcast_to(slot_column, (rows, block)) - s
        pick = (lax.broadcasted_iota(jnp.int32, (rows, block), 1) == here).astype(f32).astype(bf16)
        values = dep_recv[s // CAP : (s + block) // CAP].reshape(block, channels)
        total = total + mm(pick, jnp.concatenate(three_parts(values), axis=1))
    dep_ref[...] = (
        total[:, :channels] + total[:, channels : 2 * channels] + total[:, 2 * channels :]
    )
    sum_0[2]()
    sum_1[1]()
    state_back(0, groups)
    sum_0[3]()
    sum_1[2]()
    halo_3[1]()
    stencil_pass(a1, sides, weights, shifts, ADJOINT, half, half)
    store = pltpu.make_async_copy(half, grad_ref, store_sem.at[0])
    store.start()
    sum_0[4]()
    sum_1[3]()
    sum_1[4]()
    store.wait()


def copy_out_kernel(count, *refs):
    sources, targets, kept = refs[:count], refs[count : 2 * count], refs[2 * count : 3 * count]
    in_sems, out_sems = refs[3 * count :]
    pieces = []
    for source, target, held in zip(sources, targets, kept):
        parts = COPY_PARTS if len(source.shape) == 3 else 1
        size = source.shape[0] // parts
        for k in range(parts):
            part = pl.ds(k * size, size)
            pieces.append((source.at[part], held.at[part], target.at[part]))
    loads = [
        pltpu.make_async_copy(source, held, in_sems.at[n])
        for n, (source, held, _) in enumerate(pieces)
    ]
    stores = [
        pltpu.make_async_copy(held, target, out_sems.at[n])
        for n, (_, held, target) in enumerate(pieces)
    ]
    for load in loads:
        load.start()
    for load, store in zip(loads, stores):
        load.wait()
        store.start()
    for store in stores:
        store.wait()


def copy_out(*arrays):
    hbm = pl.BlockSpec(memory_space=pl.ANY)
    count = len(arrays)
    sems = pltpu.SemaphoreType.DMA((COPY_PARTS + count - 1,))
    return pl.pallas_call(
        functools.partial(copy_out_kernel, count),
        out_shape=tuple(jax.ShapeDtypeStruct(a.shape, a.dtype) for a in arrays),
        in_specs=[hbm] * count,
        out_specs=(hbm,) * count,
        scratch_shapes=[pltpu.VMEM(a.shape, a.dtype) for a in arrays] + [sems, sems],
    )(*arrays)


def on_device(
    start_state, coefficients, w_in, w_out, jacobian, sigma, obs_values, owner, stencil, counts
):
    tlat, feat, width = start_state.shape
    rows, channels = obs_values.shape
    hid = w_in.shape[1]
    devices = lax.axis_size("lat") * lax.axis_size("lon")
    slots = devices * CAP
    cell_count = tlat * width
    assert cell_count <= 1 << 15 and 2 * tlat <= width and max(width, channels) <= 256
    side_rows = hid * feat // (2 * width)
    share = side_rows // (devices // 2)
    assert side_rows % (devices // 2) == 0 and width % CAP == 0
    assert channels == width and hid % (2 * width) == 0 and lax.axis_size("lat") % 2 == 0
    span = PICK_ROWS * width
    keep = cell_count * slots * 2 <= PICK_BYTES
    store_shape = (
        (tlat // PICK_ROWS, max(hid, span), max(slots, span))
        if keep
        else (1, 16, width)
    )
    field = pltpu.VMEM((tlat + 2, feat, width), f32)
    shape = lambda *dims: jax.ShapeDtypeStruct(dims, f32)
    vmem = pl.BlockSpec(memory_space=pltpu.VMEM)
    hbm = pl.BlockSpec(memory_space=pl.ANY)
    dma = pltpu.SemaphoreType.DMA
    args = (
        start_state,
        coefficients,
        w_in,
        w_out.T,
        jacobian.T,
        sigma.reshape(1, channels),
        obs_values,
        owner.T,
        stencil.T,
        counts.reshape(1, rows),
    )
    grad_state, departures, grad_w_in, grad_w_out_t = pl.pallas_call(
        window_kernel,
        out_shape=(
            shape(tlat, feat, width),
            shape(rows, channels),
            shape(feat, hid),
            shape(feat, hid),
        ),
        in_specs=[hbm] + [vmem] * (len(args) - 1),
        out_specs=(hbm, vmem, vmem, vmem),
        scratch_shapes=[field] * 4
        + [
            pltpu.VMEM((tlat, feat, width), f32),
            pltpu.VMEM((4, feat, width), f32),
            pltpu.VMEM((4, feat, width), f32),
            pltpu.VMEM((4, feat, width), f32),
            pltpu.VMEM((feat, width), f32),
            pltpu.VMEM((5, feat, width), f32),
            pltpu.VMEM((2 * width, 2 * width), bf16),
            pltpu.VMEM((tlat // BACK_ROWS, hid, BACK_ROWS * width), f32),
            pltpu.VMEM((tlat // BACK_ROWS, hid, BACK_ROWS * width), f32),
            pltpu.VMEM((hid, feat), bf16),
            pltpu.VMEM((hid, feat), bf16),
            pltpu.VMEM((8, rows), jnp.int32),
            pltpu.VMEM((devices, CAP + META, width), f32),
            pltpu.VMEM((devices, CAP + META, width), f32),
            pltpu.VMEM((META, slots), jnp.int32),
            pltpu.VMEM(store_shape, bf16),
            pltpu.VMEM((2 * feat, slots), f32),
            pltpu.VMEM((2 * feat, slots), bf16),
            pltpu.VMEM((devices, CAP, channels), f32),
            pltpu.VMEM((devices, CAP, channels), f32),
            pltpu.VMEM((feat, hid), f32),
            pltpu.VMEM((feat, hid), f32),
            pltpu.VMEM((2, 2, side_rows, width), f32),
            pltpu.VMEM((2, side_rows, width), f32),
            pltpu.VMEM((2, devices // 2, share, width), f32),
            pltpu.VMEM((2, devices // 2, share, width), f32),
            pltpu.VMEM((2, share, width), f32),
            pltpu.VMEM((2, devices // 2, share, width), f32),
            pltpu.VMEM((2, 2, side_rows, width), f32),
            dma((1,)),
            dma((1,)),
            dma((4, 4)),
            dma((4, 4)),
        ]
        + [dma((devices,))] * 4
        + [dma((2, 2))] * 2
        + [dma((2, devices // 2))] * 4,
        compiler_params=pltpu.CompilerParams(
            collective_id=0, has_side_effects=True, vmem_limit_bytes=VMEM_LIMIT
        ),
    )(*args)
    grad_state, departures, grad_w_in, grad_w_out_t = copy_out(
        grad_state, departures, grad_w_in, grad_w_out_t
    )
    return grad_state, departures, grad_w_in, grad_w_out_t.T


def solution(mesh):
    return jax.shard_map(
        on_device,
        mesh=mesh,
        in_specs=(
            P("lat", None, "lon"),
            P(),
            P(),
            P(),
            P(),
            P(),
            P(("lat", "lon"), None),
            P(("lat", "lon"), None),
            P(("lat", "lon"), None),
            P(("lat", "lon")),
        ),
        out_specs=(P("lat", None, "lon"), P(("lat", "lon"), None), P(), P()),
        check_vma=False,
    )
```

```python
import functools
import math

import jax
import jax.numpy as jnp
from jax import lax
from jax.experimental import pallas as pl
from jax.experimental.pallas import tpu as pltpu
from jax.sharding import PartitionSpec as P

CAP = 16
CLOSURE_ROWS = 16
BACK_ROWS = 8
PICK_ROWS = 4
PASS_ROWS = 32
COPY_PARTS = 16
BACK_UNROLL, PICK_UNROLL, PASS_UNROLL, CLOSURE_UNROLL = 4, 8, 4, 2
SLOT_BLOCK = 512
META = 8
VMEM_LIMIT = 60 * 1024 * 1024
PICK_BYTES = 10 * 1024 * 1024
corner_tenths = (4, 3, 2, 1)
TENTH = 0.1
FORWARD, ADJOINT = (0, 1, 2, 3, 4), (0, 2, 1, 4, 3)
bf16, f32 = jnp.bfloat16, jnp.float32


def mm(a, b):
    return jnp.dot(a, b, preferred_element_type=f32)


def mm_nt(a, b, precision=None):
    return lax.dot_general(
        a, b, (((1,), (1,)), ((), ())), precision=precision, preferred_element_type=f32
    )


def two_parts(x):
    high = x.astype(bf16)
    low = (x - high.astype(f32)).astype(bf16)
    return high, low


def three_parts(x):
    high = x.astype(bf16)
    rest = x - high.astype(f32)
    middle = rest.astype(bf16)
    low = (rest - middle.astype(f32)).astype(bf16)
    return high, middle, low


def turn(x):
    return jnp.transpose(x.astype(f32)).astype(x.dtype)


def picks(local, cells):
    slots = local.shape[1]
    low = local.astype(jnp.int16)
    cell = lax.broadcasted_iota(jnp.int16, (cells, slots), 0)
    zero = jnp.zeros((cells, slots), bf16)
    pick = zero
    for k in range(4):
        same = cell == jnp.broadcast_to(low[k : k + 1], (cells, slots))
        pick = pick + jnp.where(same, jnp.full_like(zero, corner_tenths[k]), zero)
    return pick


def gather_rows(ref, base, count):
    return jnp.concatenate([ref[base + g + 1] for g in range(count)], axis=1).astype(bf16)


def merge_edges(from_west, from_east):
    feat, width = from_west.shape
    lane = lax.broadcasted_iota(jnp.int32, (feat, width), 1)
    return jnp.where(
        lane % 2 == 0, pltpu.roll(from_east, width - 1, axis=1), pltpu.roll(from_west, 1, axis=1)
    )


def edge_pass(field, edge):
    rows, feat, width = field.shape
    pair = lax.broadcasted_iota(jnp.int32, (8, width), 1) >> 1

    def step(b, carry):
        part = pl.ds(pl.multiple_of(b * 8, 8), 8)
        kept = []
        for first in range(0, rows - 2, PASS_ROWS):
            total = jnp.zeros((8, width), f32)
            for i in range(first, first + PASS_ROWS):
                moved = pltpu.roll(field[i + 1, part], 2 * i + 1, axis=1)
                total = jnp.where(pair == i, moved, total)
            kept.append(total)
        edge[part] = sum(kept)
        return carry

    lax.fori_loop(0, feat // 8, step, 0, unroll=PASS_UNROLL)


def shift_matrix(width):
    row = lax.broadcasted_iota(jnp.int32, (2 * width, 2 * width), 0) % width
    column = lax.broadcasted_iota(jnp.int32, (2 * width, 2 * width), 1)
    taken = jnp.where(column < width, column - 1, column - width + 1)
    return (row == taken).astype(f32).astype(bf16)


def stencil_pass(field, sides, weights, shifts, order, base, out, edge=None, shift=0):
    rows, feat, width = field.shape
    lane = lax.broadcasted_iota(jnp.int32, (8, width), 1)
    pair = lane >> 1

    def step(b, carry):
        part = pl.ds(pl.multiple_of(b * 8, 8), 8)
        centre, north, south, west, east = [weights[k, part] for k in order]
        ends = jnp.where(lane == 0, west, jnp.where(lane == width - 1, east, 0.0))
        side = sides[part]
        inner = field[1 : rows - 1, part].reshape((rows - 2) * 8, width)
        beside = mm(jnp.concatenate(two_parts(inner), axis=1), shifts[...])

        def read(start):
            fresh = range(start, min(start + PASS_ROWS, rows - 2))
            return [field[i + 2, part] for i in fresh], [base[i + shift, part] for i in fresh]

        before, here = field[0, part], field[1, part]
        kept = []
        ready = read(0)
        for start in range(0, rows - 2, PASS_ROWS):
            afters, bases = ready
            ready = read(start + PASS_ROWS)
            results = []
            for i, after, total in zip(range(start, start + PASS_ROWS), afters, bases):
                near = beside[i * 8 : (i + 1) * 8]
                results.append(
                    total
                    + centre * here
                    + north * before
                    + south * after
                    + west * near[:, :width]
                    + east * near[:, width:]
                    + ends * pltpu.roll(side, width - 1 - 2 * i, axis=1)
                )
                before, here = here, after
            for g, row in enumerate(results):
                out[start + g + shift, part] = row
            if edge is not None:
                total = jnp.zeros((8, width), f32)
                for g, row in enumerate(results):
                    i = start + g
                    total = jnp.where(pair == i, pltpu.roll(row, 2 * i + 1, axis=1), total)
                kept.append(total)
        if edge is not None:
            edge[part] = sum(kept)
        return carry

    lax.fori_loop(0, feat // 8, step, 0, unroll=PASS_UNROLL)


def remote(src, dst, send, recv, to):
    return pltpu.make_async_remote_copy(
        src_ref=src,
        dst_ref=dst,
        send_sem=send,
        recv_sem=recv,
        device_id=to,
        device_id_type=pl.DeviceIdType.MESH,
    )


def window_kernel(
    start_ref,
    coef_ref,
    w_in_ref,
    w_out_t_ref,
    jac_t_ref,
    sigma_ref,
    obs_ref,
    owner_ref,
    stencil_ref,
    counts_ref,
    grad_ref,
    dep_ref,
    gin_out,
    gout_out,
    x0,
    x1,
    a2,
    a1,
    half,
    edges,
    from_west,
    from_east,
    sides,
    weights,
    shifts,
    tanh_0,
    tanh_1,
    w_in_t,
    w_out,
    slot_row,
    obs_send,
    obs_recv,
    cells,
    pick_store,
    acc,
    parts,
    dep_send,
    dep_recv,
    gin,
    gout,
    pair_send,
    pair_recv,
    rs_send,
    rs_recv,
    ag_send,
    ag_recv,
    whole,
    load_sem,
    store_sem,
    halo_send,
    halo_recv,
    obs_ssem,
    obs_rsem,
    dep_ssem,
    dep_rsem,
    pair_ssem,
    pair_rsem,
    rs_ssem,
    rs_rsem,
    ag_ssem,
    ag_rsem,
):
    tlat, feat, width = start_ref.shape
    hid = w_in_ref.shape[1]
    rows, channels = obs_ref.shape
    slots = cells.shape[1]
    block = min(slots, SLOT_BLOCK)
    lat, lon = lax.axis_index("lat"), lax.axis_index("lon")
    lats, lons = lax.axis_size("lat"), lax.axis_size("lon")
    devices = lats * lons
    me = lat * lons + lon
    south, north = {"lat": lax.rem(lat + 1, lats)}, {"lat": lax.rem(lat + lats - 1, lats)}
    east, west = {"lon": lax.rem(lon + 1, lons)}, {"lon": lax.rem(lon + lons - 1, lons)}

    load = pltpu.make_async_copy(start_ref, x0.at[pl.ds(1, tlat)], load_sem.at[0])
    load.start()

    def place(index):
        return {"lat": index // lons, "lon": lax.rem(index, lons)}

    barrier = pltpu.get_barrier_semaphore()

    def greet(k, carry):
        pl.semaphore_signal(
            barrier,
            inc=1,
            device_id=place(lax.rem(me + k, devices)),
            device_id_type=pl.DeviceIdType.MESH,
        )
        return carry

    lax.fori_loop(1, devices, greet, 0)

    def swap(source, target, send, recv, spread=False, own=me, count=devices, place=place):
        def copy_to(k):
            peer = lax.rem(own + k, count)
            return remote(
                source if spread else source.at[peer],
                target.at[own],
                send.at[k],
                recv.at[k],
                place(peer),
            )

        def start():
            def body(k, carry):
                copy_to(k).start()
                return carry

            lax.fori_loop(1, count, body, 0)
            target[own] = source[...] if spread else source[own]

        def finish():
            def body(k, carry):
                copy_to(k).wait()
                return carry

            lax.fori_loop(1, count, body, 0)

        return start, finish

    def halo(number, field):
        sources = (
            (field.at[tlat], field.at[0], south),
            (field.at[1], field.at[tlat + 1], north),
            (edges.at[number], from_west.at[number], east),
            (edges.at[number], from_east.at[number], west),
        )
        copies = [
            remote(src, dst, halo_send.at[number, k], halo_recv.at[number, k], to)
            for k, (src, dst, to) in enumerate(sources)
        ]

        def start():
            for copy in copies:
                copy.start()

        def finish():
            for copy in copies:
                copy.wait()

            @pl.when(lat == 0)
            def _():
                field[0] = jnp.zeros((feat, width), f32)

            @pl.when(lat == lats - 1)
            def _():
                field[tlat + 1] = jnp.zeros((feat, width), f32)

            sides[...] = merge_edges(from_west[number], from_east[number])

        return start, finish

    owner = owner_ref[...]
    tile = lax.broadcasted_iota(jnp.int32, (devices, rows), 0)
    named = (tile == jnp.broadcast_to(owner, (devices, rows))).astype(f32)
    earlier = (
        lax.broadcasted_iota(jnp.int32, (rows, rows), 0)
        < lax.broadcasted_iota(jnp.int32, (rows, rows), 1)
    ).astype(f32)
    before = mm(named.astype(bf16), earlier.astype(bf16))
    rank = jnp.sum(named * before, axis=0, keepdims=True)
    slot = owner * CAP + rank.astype(jnp.int32)
    slot_row[...] = jnp.broadcast_to(slot, slot_row.shape)
    w_in_t[...] = turn(w_in_ref[...])
    w_out[...] = turn(w_out_t_ref[...])

    obs_parts = jnp.concatenate(three_parts(obs_ref[...]), axis=1)
    stencil = stencil_ref[...]
    filler = jnp.zeros((META - 5, rows), f32)
    meta = jnp.concatenate(
        [
            (stencil // width).astype(f32),
            counts_ref[...].astype(f32),
            filler,
            (stencil % width).astype(f32),
            jnp.zeros((META - 4, rows), f32),
        ],
        axis=0,
    ).astype(bf16)
    per_group = width // CAP
    for s in range(0, slots, block):
        here = jnp.broadcast_to(slot, (block, rows)) - s
        pick = (lax.broadcasted_iota(jnp.int32, (block, rows), 0) == here).astype(f32).astype(bf16)
        wide = mm(pick, obs_parts)
        values = wide[:, :channels] + wide[:, channels : 2 * channels] + wide[:, 2 * channels :]
        for t in range(block // CAP):
            obs_send[s // CAP + t, :CAP] = values[t * CAP : (t + 1) * CAP]
        both = mm_nt(meta, pick)
        scale = jnp.where(
            lax.broadcasted_iota(jnp.int32, (META, block), 0) < 4, float(width), 1.0
        )
        lines = both[:META] * scale + both[META:]
        for t in range(block // CAP):
            g = t // per_group
            line = lines[:, g * width : (g + 1) * width]
            shift = (width - (t % per_group) * CAP) % width
            obs_send[s // CAP + t, CAP:] = pltpu.roll(line, shift, axis=1) if shift else line

    load.wait()
    edge_pass(x0, edges.at[0])
    shifts[...] = shift_matrix(width)
    turned = jnp.transpose(coef_ref[...])
    for k in range(5):
        weights[k] = jnp.broadcast_to(turned[:, k : k + 1], (feat, width))

    pl.semaphore_wait(barrier, devices - 1)
    halo_0, halo_1 = halo(0, x0), halo(1, x1)
    halo_2, halo_3 = halo(2, a2), halo(3, a1)
    halo_0[0]()
    obs_start, obs_finish = swap(obs_send, obs_recv, obs_ssem, obs_rsem)
    obs_start()

    per_step = CLOSURE_ROWS // BACK_ROWS

    def closure(field, kept, out, shift):
        def step(b, carry):
            base = b * CLOSURE_ROWS
            inputs = gather_rows(field, base, CLOSURE_ROWS)
            tanh_pre = jnp.tanh(mm(w_in_t[...], inputs))
            for g in range(per_step):
                columns = slice(g * BACK_ROWS * width, (g + 1) * BACK_ROWS * width)
                kept[b * per_step + g] = tanh_pre[:, columns]
            result = mm(w_out_t_ref[...], tanh_pre.astype(bf16))
            for g in range(CLOSURE_ROWS):
                out[base + g + shift] = result[:, g * width : (g + 1) * width]
            return carry

        lax.fori_loop(0, tlat // CLOSURE_ROWS, step, 0, unroll=CLOSURE_UNROLL)

    closure(x0, tanh_0, x1, 1)
    halo_0[1]()
    stencil_pass(x0, sides, weights, shifts, FORWARD, x1, x1, edges.at[1], 1)
    halo_1[0]()

    closure(x1, tanh_1, half, 0)
    halo_1[1]()
    stencil_pass(x1, sides, weights, shifts, FORWARD, half, half)
    obs_finish()
    lane = lax.broadcasted_iota(jnp.int32, (META, width), 1)
    for g in range(devices // per_group):
        line = obs_recv[g * per_group, CAP:]
        for t in range(1, per_group):
            moved = pltpu.roll(obs_recv[g * per_group + t, CAP:], t * CAP, axis=1)
            line = jnp.where(lane >= t * CAP, moved, line)
        cells[:, g * width : (g + 1) * width] = line.astype(jnp.int32)
    acc[...] = jnp.zeros_like(acc)
    keep = tlat * width * slots * 2 <= PICK_BYTES

    def interpolate(b, carry):
        base = b * PICK_ROWS
        state = jnp.concatenate([half[base + g] for g in range(PICK_ROWS)], axis=1)
        both = jnp.concatenate(two_parts(state), axis=0)
        for s in range(0, slots, block):
            pick = picks(cells[:, s : s + block] - base * width, PICK_ROWS * width)
            if keep:
                pick_store[b, : PICK_ROWS * width, s : s + block] = pick
            acc[:, s : s + block] += mm(both, pick)
        return carry

    lax.fori_loop(0, tlat // PICK_ROWS, interpolate, 0, unroll=PICK_UNROLL)

    jac_t = jac_t_ref[...]
    sigma = sigma_ref[...]
    for s in range(0, slots, block):
        interp = jnp.transpose((acc[:feat, s : s + block] + acc[feat:, s : s + block]) * TENTH)
        evolved = jnp.dot(
            interp, jac_t, precision=lax.Precision.HIGHEST, preferred_element_type=f32
        )
        counts = jnp.transpose(cells[:, s : s + block].astype(f32))[:, 4:5]
        channel = lax.broadcasted_iota(jnp.int32, (block, channels), 1).astype(f32)
        used = channel < jnp.broadcast_to(counts, (block, channels))
        obs = obs_recv[s // CAP : (s + block) // CAP, :CAP].reshape(block, channels)
        departures = jnp.where(used, (obs - evolved) / sigma, 0.0)
        dep_send[s // CAP : (s + block) // CAP] = departures.reshape(block // CAP, CAP, channels)
        pulled = mm_nt(jac_t, -departures / sigma, lax.Precision.HIGHEST)
        parts[:, s : s + block] = jnp.concatenate(two_parts(pulled * TENTH), axis=0)
    dep_start, dep_finish = swap(dep_send, dep_recv, dep_ssem, dep_rsem)
    dep_start()

    def spread(b, carry):
        base = b * PICK_ROWS
        total = jnp.zeros((2 * feat, PICK_ROWS * width), f32)
        for s in range(0, slots, block):
            if keep:
                pick = pick_store[b, : PICK_ROWS * width, s : s + block]
            else:
                pick = picks(cells[:, s : s + block] - base * width, PICK_ROWS * width)
            total = total + mm_nt(parts[:, s : s + block], pick)
        out = total[:feat] + total[feat:]
        for g in range(PICK_ROWS):
            a2[base + g + 1] = out[:, g * width : (g + 1) * width]
        return carry

    lax.fori_loop(0, tlat // PICK_ROWS, spread, 0, unroll=PICK_UNROLL)
    edge_pass(a2, edges.at[2])
    halo_2[0]()

    gin[...] = jnp.zeros_like(gin)
    gout[...] = jnp.zeros_like(gout)

    def closure_back(state, kept, cot_field, out, shift):
        def step(b, carry):
            base = b * BACK_ROWS
            inputs = gather_rows(state, base, BACK_ROWS)
            cot = gather_rows(cot_field, base, BACK_ROWS)
            tanh_pre = kept[b]
            gout[...] += mm_nt(tanh_pre.astype(bf16), cot)
            back_hidden = mm(w_out[...], cot)
            back_pre = (back_hidden * (1.0 - tanh_pre * tanh_pre)).astype(bf16)
            gin[...] += mm_nt(inputs, back_pre)
            back = mm(w_in_ref[...], back_pre)
            for g in range(BACK_ROWS):
                out[base + g + shift] = back[:, g * width : (g + 1) * width]
            return carry

        lax.fori_loop(0, tlat // BACK_ROWS, step, 0, unroll=BACK_UNROLL)

    closure_back(x1, tanh_1, a2, a1, 1)
    halo_2[1]()
    stencil_pass(a2, sides, weights, shifts, ADJOINT, a1, a1, edges.at[3], 1)
    halo_3[0]()

    side = lax.rem(lat, 2)
    partner = {"lat": lat + 1 - 2 * side}
    pairs = devices // 2
    pair = (lat // 2) * lons + lon
    scale = 1.0 / math.sqrt(tlat * lats * width * lons)
    groups = tlat // BACK_ROWS
    per_group_picks = BACK_ROWS // PICK_ROWS
    span = PICK_ROWS * width
    depth = hid // 2

    def pair_place(index):
        return {"lat": (index // lons) * 2 + side, "lon": lax.rem(index, lons)}

    def half_sum(c):
        first = remote(
            pair_send.at[c, 1 - side],
            pair_recv.at[c],
            pair_ssem.at[c, 0],
            pair_rsem.at[c, 0],
            partner,
        )
        last = remote(
            whole.at[c, side],
            whole.at[c, side],
            pair_ssem.at[c, 1],
            pair_rsem.at[c, 1],
            partner,
        )
        group = dict(own=pair, count=pairs, place=pair_place)
        scatter = swap(rs_send.at[c], rs_recv.at[c], rs_ssem.at[c], rs_rsem.at[c], **group)
        gather = swap(
            ag_send.at[c], ag_recv.at[c], ag_ssem.at[c], ag_rsem.at[c], spread=True, **group
        )

        def begin():
            columns = slice(c * depth, (c + 1) * depth)
            grads = jnp.concatenate([gin[:, columns], jnp.transpose(gout[columns])], axis=0)
            stacked = jnp.concatenate(
                [grads[:, k : k + width] for k in range(0, depth, width)], axis=0
            )
            pair_send[c] = stacked.reshape(pair_send.shape[1:])
            first.start()

        def reduce():
            first.wait()
            rs_send[c] = (pair_send[c, side] + pair_recv[c]).reshape(rs_send.shape[1:])
            scatter[0]()

        def share():
            scatter[1]()
            ag_send[c] = jnp.sum(rs_recv[c], axis=0) * scale
            gather[0]()

        def exchange():
            gather[1]()
            whole[c, side] = ag_recv[c].reshape(whole.shape[2:])
            last.start()

        def end():
            last.wait()
            tiles = whole[c].reshape(depth // width, 2 * feat, width)
            for k in range(depth // width):
                columns = slice(c * depth + k * width, c * depth + (k + 1) * width)
                gin_out[:, columns] = tiles[k, :feat]
                gout_out[:, columns] = tiles[k, feat:]

        return begin, reduce, share, exchange, end

    def half_back(c, first, last):
        units = slice(c * depth, (c + 1) * depth)

        def step(b, carry):
            base = b * BACK_ROWS
            inputs = gather_rows(x0, base, BACK_ROWS)
            cot = gather_rows(a1, base, BACK_ROWS)
            tanh_pre = tanh_0[b, units]
            gout[units] += mm_nt(tanh_pre.astype(bf16), cot)
            back_hidden = mm(w_out[units], cot)
            back_pre = (back_hidden * (1.0 - tanh_pre * tanh_pre)).astype(bf16)
            gin[:, units] += mm_nt(inputs, back_pre)
            if keep:
                for k in range(per_group_picks):
                    pick_store[b * per_group_picks + k, units, :span] = back_pre[
                        :, k * span : (k + 1) * span
                    ]
            else:
                tanh_1[b, units] = back_pre.astype(f32)
            return carry

        lax.fori_loop(first, last, step, 0, unroll=BACK_UNROLL)

    def state_back(first, last):
        def step(b, carry):
            if keep:
                back_pre = jnp.concatenate(
                    [
                        pick_store[b * per_group_picks + k, :hid, :span]
                        for k in range(per_group_picks)
                    ],
                    axis=1,
                )
            else:
                back_pre = tanh_1[b].astype(bf16)
            back = mm(w_in_ref[...], back_pre)
            for g in range(BACK_ROWS):
                half[b * BACK_ROWS + g] = back[:, g * width : (g + 1) * width]
            return carry

        lax.fori_loop(first, last, step, 0, unroll=BACK_UNROLL)

    sum_0, sum_1 = half_sum(0), half_sum(1)
    half_back(0, 0, groups)
    sum_0[0]()
    half_back(1, 0, groups // 2)
    sum_0[1]()
    half_back(1, groups // 2, groups)
    sum_1[0]()
    dep_finish()
    slot_column = jnp.transpose(slot_row[...].astype(f32))[:, :1].astype(jnp.int32)
    total = jnp.zeros((rows, 3 * channels), f32)
    for s in range(0, slots, block):
        here = jnp.broadcast_to(slot_column, (rows, block)) - s
        pick = (lax.broadcasted_iota(jnp.int32, (rows, block), 1) == here).astype(f32).astype(bf16)
        values = dep_recv[s // CAP : (s + block) // CAP].reshape(block, channels)
        total = total + mm(pick, jnp.concatenate(three_parts(values), axis=1))
    dep_ref[...] = (
        total[:, :channels] + total[:, channels : 2 * channels] + total[:, 2 * channels :]
    )
    sum_1[1]()
    sum_0[2]()
    state_back(0, groups)
    sum_1[2]()
    sum_0[3]()
    halo_3[1]()
    stencil_pass(a1, sides, weights, shifts, ADJOINT, half, half)
    store = pltpu.make_async_copy(half, grad_ref, store_sem.at[0])
    store.start()
    sum_0[4]()
    sum_1[3]()
    sum_1[4]()
    store.wait()


def copy_out_kernel(count, *refs):
    sources, targets, kept = refs[:count], refs[count : 2 * count], refs[2 * count : 3 * count]
    in_sems, out_sems = refs[3 * count :]
    pieces = []
    for source, target, held in zip(sources, targets, kept):
        parts = COPY_PARTS if len(source.shape) == 3 else 1
        size = source.shape[0] // parts
        for k in range(parts):
            part = pl.ds(k * size, size)
            pieces.append((source.at[part], held.at[part], target.at[part]))
    loads = [
        pltpu.make_async_copy(source, held, in_sems.at[n])
        for n, (source, held, _) in enumerate(pieces)
    ]
    stores = [
        pltpu.make_async_copy(held, target, out_sems.at[n])
        for n, (_, held, target) in enumerate(pieces)
    ]
    for load in loads:
        load.start()
    for load, store in zip(loads, stores):
        load.wait()
        store.start()
    for store in stores:
        store.wait()


def copy_out(*arrays):
    hbm = pl.BlockSpec(memory_space=pl.ANY)
    count = len(arrays)
    sems = pltpu.SemaphoreType.DMA((COPY_PARTS + count - 1,))
    return pl.pallas_call(
        functools.partial(copy_out_kernel, count),
        out_shape=tuple(jax.ShapeDtypeStruct(a.shape, a.dtype) for a in arrays),
        in_specs=[hbm] * count,
        out_specs=(hbm,) * count,
        scratch_shapes=[pltpu.VMEM(a.shape, a.dtype) for a in arrays] + [sems, sems],
    )(*arrays)


def on_device(
    start_state, coefficients, w_in, w_out, jacobian, sigma, obs_values, owner, stencil, counts
):
    tlat, feat, width = start_state.shape
    rows, channels = obs_values.shape
    hid = w_in.shape[1]
    devices = lax.axis_size("lat") * lax.axis_size("lon")
    slots = devices * CAP
    cell_count = tlat * width
    assert cell_count <= 1 << 15 and 2 * tlat <= width and max(width, channels) <= 256
    side_rows = hid * feat // (2 * width)
    share = side_rows // (devices // 2)
    assert side_rows % (devices // 2) == 0 and width % CAP == 0
    assert channels == width and hid % (2 * width) == 0 and lax.axis_size("lat") % 2 == 0
    span = PICK_ROWS * width
    keep = cell_count * slots * 2 <= PICK_BYTES
    store_shape = (
        (tlat // PICK_ROWS, max(hid, span), max(slots, span))
        if keep
        else (1, 16, width)
    )
    field = pltpu.VMEM((tlat + 2, feat, width), f32)
    shape = lambda *dims: jax.ShapeDtypeStruct(dims, f32)
    vmem = pl.BlockSpec(memory_space=pltpu.VMEM)
    hbm = pl.BlockSpec(memory_space=pl.ANY)
    dma = pltpu.SemaphoreType.DMA
    args = (
        start_state,
        coefficients,
        w_in,
        w_out.T,
        jacobian.T,
        sigma.reshape(1, channels),
        obs_values,
        owner.T,
        stencil.T,
        counts.reshape(1, rows),
    )
    grad_state, departures, grad_w_in, grad_w_out_t = pl.pallas_call(
        window_kernel,
        out_shape=(
            shape(tlat, feat, width),
            shape(rows, channels),
            shape(feat, hid),
            shape(feat, hid),
        ),
        in_specs=[hbm] + [vmem] * (len(args) - 1),
        out_specs=(hbm, vmem, vmem, vmem),
        scratch_shapes=[field] * 4
        + [
            pltpu.VMEM((tlat, feat, width), f32),
            pltpu.VMEM((4, feat, width), f32),
            pltpu.VMEM((4, feat, width), f32),
            pltpu.VMEM((4, feat, width), f32),
            pltpu.VMEM((feat, width), f32),
            pltpu.VMEM((5, feat, width), f32),
            pltpu.VMEM((2 * width, 2 * width), bf16),
            pltpu.VMEM((tlat // BACK_ROWS, hid, BACK_ROWS * width), f32),
            pltpu.VMEM((tlat // BACK_ROWS, hid, BACK_ROWS * width), f32),
            pltpu.VMEM((hid, feat), bf16),
            pltpu.VMEM((hid, feat), bf16),
            pltpu.VMEM((8, rows), jnp.int32),
            pltpu.VMEM((devices, CAP + META, width), f32),
            pltpu.VMEM((devices, CAP + META, width), f32),
            pltpu.VMEM((META, slots), jnp.int32),
            pltpu.VMEM(store_shape, bf16),
            pltpu.VMEM((2 * feat, slots), f32),
            pltpu.VMEM((2 * feat, slots), bf16),
            pltpu.VMEM((devices, CAP, channels), f32),
            pltpu.VMEM((devices, CAP, channels), f32),
            pltpu.VMEM((feat, hid), f32),
            pltpu.VMEM((hid, feat), f32),
            pltpu.VMEM((2, 2, side_rows, width), f32),
            pltpu.VMEM((2, side_rows, width), f32),
            pltpu.VMEM((2, devices // 2, share, width), f32),
            pltpu.VMEM((2, devices // 2, share, width), f32),
            pltpu.VMEM((2, share, width), f32),
            pltpu.VMEM((2, devices // 2, share, width), f32),
            pltpu.VMEM((2, 2, side_rows, width), f32),
            dma((1,)),
            dma((1,)),
            dma((4, 4)),
            dma((4, 4)),
        ]
        + [dma((devices,))] * 4
        + [dma((2, 2))] * 2
        + [dma((2, devices // 2))] * 4,
        compiler_params=pltpu.CompilerParams(
            collective_id=0, has_side_effects=True, vmem_limit_bytes=VMEM_LIMIT
        ),
    )(*args)
    grad_state, departures, grad_w_in, grad_w_out_t = copy_out(
        grad_state, departures, grad_w_in, grad_w_out_t
    )
    return grad_state, departures, grad_w_in, grad_w_out_t.T


def solution(mesh):
    return jax.shard_map(
        on_device,
        mesh=mesh,
        in_specs=(
            P("lat", None, "lon"),
            P(),
            P(),
            P(),
            P(),
            P(),
            P(("lat", "lon"), None),
            P(("lat", "lon"), None),
            P(("lat", "lon"), None),
            P(("lat", "lon")),
        ),
        out_specs=(P("lat", None, "lon"), P(("lat", "lon"), None), P(), P()),
        check_vma=False,
    )
```
